512 devices in a mesh: freq: 64 (over y_hi, x, z), cuts: 8 (over y_lo, core).
Axes of the slice: x: 4, y: 8 (y_hi: 2, y_lo: 4; y = y_hi * 4 + y_lo), z: 8, core: 2. Of those that a mesh axis runs over, the one named last changes fastest.
Arguments:
- wavefield: bfloat16 [64, 2, 2048, 2048], P('freq', None, 'cuts'), may hold values from -6 to 6
- slowness: bfloat16 [64, 2048, 2048], P('freq', 'cuts'), may hold values from 0.25 to 0.546875
- block_inverse: bfloat16 [64, 2, 40, 64, 64], P('freq', None, 'cuts'), may hold values from -0.75 to 0.75
- block_lengths: int32 [64, 40], replicated, may hold values from 1 to 64, 2048 in all within a row
- slab_owner: int32 [1], replicated, may hold values from 0 to 63
- shot_position: int32 [2], replicated, may hold values from 0 to 2047
Outputs:
- image: float32 [1, 2048, 2048], P(None, 'cuts', 'freq')
The draws below stay inside these ranges and needn't reach their ends.
Inputs may be any that keep to these rules, and one draw needn't show every extreme that they name: `block_lengths`: each row lists the lengths of the 40 blocks of a line in order; they sum to 2048 and the longest is exactly 64.
All inputs are finite; a program needn't handle non-finite values.
Results may differ from the reference program's by a relative error of at most 0.012.
Values may be sent and summed in bfloat16 or wider, within the bound.
No kernel may reach another device: no remote copies, remote signals or barrier semaphores. Data moves between devices by JAX's collectives and lax.ppermute only.
A program may use at most 64 MiB of HBM per device.

```python
import math
import jax
import jax.numpy as jnp
import numpy as np
from jax import lax

NX = 2048
NY = 2048
B = 64
C = 40
STEPS = 1
FREQS = 64


def shard_levels(stream_key, dims, split, smallest, largest):
    def one(dim, parts):
        heights = jax.random.uniform(jax.random.fold_in(jax.random.fold_in(stream_key, 6), dim), (parts,), jnp.float32, smallest / len(split), largest / len(split))
        return jnp.repeat(jnp.exp(heights), dims[dim] // parts).reshape((-1,) + (1,) * (len(dims) - dim - 1))

    gain = one(*split[0])
    for cut in split[1:]:
        gain = gain * one(*cut)
    return gain


def length_profile(number_of, total, most, lean):
    portions = [(1 << 20) // math.isqrt(standing ** lean) + 1 for standing in range(2, number_of + 1)]
    rest, counts = total - most - (number_of - 1), [1] * (number_of - 1)
    while rest > 0:
        candidates = [i for i in range(number_of - 1) if counts[i] < most]
        mass, left = sum([portions[i] for i in candidates]), rest
        for i in candidates:
            more = min(most - counts[i], max(1, left * portions[i] // mass), rest)
            counts[i] = counts[i] + more
            rest = rest - more
    return np.array([most] + counts)


def uneven(rng, number_of, total, reach, skew):
    if number_of == 2:
        one = jax.random.randint(rng, (), max(1, total - reach), min(reach, total - 1) + 1)
        return jnp.stack([one, total - one])
    lengths = jnp.asarray(length_profile(number_of, total, reach, skew), jnp.int32)
    twos = (number_of - 1) // 2
    donor, sink = lengths[1:1 + 2 * twos:2], lengths[2:2 + 2 * twos:2]
    margin = jnp.minimum(donor - 1, reach - sink)
    passed = jax.random.randint(jax.random.fold_in(rng, 1), (twos,), 0, 1 << 20) % (margin + 1)
    lengths = lengths.at[1:1 + 2 * twos:2].set(donor - passed).at[2:2 + 2 * twos:2].set(sink + passed)
    return lengths[jax.random.permutation(jax.random.fold_in(rng, 2), number_of)]


def bell_draw(own_key, shape, width, bound, split=(), kind=jnp.bfloat16):
    drawn = width * jax.random.normal(own_key, shape, jnp.float32)
    if split:
        drawn = drawn * shard_levels(own_key, shape, split, -0.22, 0.18)
    return jnp.clip(drawn, -bound, bound).astype(kind)


def setup_inputs(seed: int = 0) -> dict:
    splits = jax.random.split(jax.random.key(seed), 7)
    return {
        "wavefield": bell_draw(splits[0], (FREQS, 2, NX, NY), 1.0, 6.0, ((0, 64), (2, 8))),
        "slowness": jnp.clip(0.25 + 0.296875 * jax.random.uniform(splits[1], (FREQS, NX, NY), jnp.float32) ** shard_levels(splits[1], (FREQS, NX, NY), ((0, 64), (1, 8)), -0.2, 0.2), 0.25, 0.546875).astype(jnp.bfloat16),
        "block_inverse": bell_draw(splits[2], (FREQS, 2, C, B, B), 0.05, 0.75, ((0, 64), (2, 8))),
        "block_lengths": jax.vmap(lambda own: uneven(own, C, NY, B, 1))(jax.random.split(splits[3], FREQS)).reshape((FREQS, C)).astype(jnp.int32),
        "slab_owner": jax.random.randint(splits[4], (STEPS,), 0, FREQS).astype(jnp.int32),
        "shot_position": jax.random.randint(splits[5], (2,), 0, min(NX, NY)).astype(jnp.int32),
    }


grid_step = 0.0125
depth_step = 0.02
slow_ref = 0.4
band_low = 5.0
band_width = 55.0
highest = lax.Precision.HIGHEST

def split_length(extent):
    outer_len = 2 ** ((extent.bit_length() - 1) // 2)
    return (outer_len, extent // outer_len)

def outer_table(outer_len, orient):
    first_ids = jnp.arange(outer_len, dtype=jnp.int32)
    indices = first_ids[:, None] * first_ids[None, :] % outer_len
    angles = orient * 2.0 * math.pi / outer_len * indices.astype(jnp.float32)
    cosine = jnp.cos(angles) / math.sqrt(outer_len)
    sine = jnp.sin(angles) / math.sqrt(outer_len)
    first = jnp.stack([cosine, sine], axis=1)
    second = jnp.stack([-sine, cosine], axis=1)
    return jnp.stack([first, second], axis=0).astype(jnp.bfloat16)

def inner_table(outer_len, inner_len, orient):
    extent = outer_len * inner_len
    outer_ids = jnp.arange(outer_len, dtype=jnp.int32)[:, None, None]
    inner_ids = jnp.arange(inner_len, dtype=jnp.int32)[None, :, None]
    freq_ids = jnp.arange(inner_len, dtype=jnp.int32)[None, None, :]
    indices = inner_ids * (outer_ids + outer_len * freq_ids) % extent
    angles = orient * 2.0 * math.pi / extent * indices.astype(jnp.float32)
    cosine = jnp.cos(angles) / math.sqrt(inner_len)
    sine = jnp.sin(angles) / math.sqrt(inner_len)
    first = jnp.stack([cosine, sine], axis=2)
    second = jnp.stack([-sine, cosine], axis=2)
    return jnp.stack([first, second], axis=2).astype(jnp.bfloat16)

def mixing(formula, operand, table):
    return jnp.einsum(formula, operand.astype(jnp.float32), table.astype(jnp.float32), precision=highest)

def forward_lines(field):
    rows = field.shape[1]
    outer_len, inner_len = split_length(field.shape[2])
    shaped = field.reshape(2, rows, outer_len, inner_len)
    first_section = mixing('cmab,cadk->mbdk', shaped, outer_table(outer_len, -1.0)).astype(jnp.bfloat16)
    return mixing('mbdk,kbdeq->kmeq', first_section, inner_table(outer_len, inner_len, -1.0)).astype(jnp.bfloat16)

def across_forward(columns):
    count_k, extent_x, _, count_q = columns.shape
    outer_len, inner_len = split_length(extent_x)
    shaped = columns.reshape(count_k, outer_len, inner_len, 2, count_q)
    first_section = mixing('kabcq,cadz->kbqdz', shaped, outer_table(outer_len, -1.0)).astype(jnp.bfloat16)
    return mixing('kbqdz,zbdwu->zkqwu', first_section, inner_table(outer_len, inner_len, -1.0))

def across_inverse(spectrum, extent_x):
    count_k = spectrum.shape[1]
    count_q = spectrum.shape[2]
    outer_len, inner_len = split_length(extent_x)
    first_section = mixing('zkqwu,zbwdu->zkqdb', spectrum, inner_table(outer_len, inner_len, 1.0)).astype(jnp.bfloat16)
    second_section = mixing('zkqdb,daez->kabeq', first_section, outer_table(outer_len, 1.0)).astype(jnp.bfloat16)
    return second_section.reshape(count_k, extent_x, 2, count_q)

def lines_inverse(spectrum, extent_y):
    rows = spectrum.shape[1]
    outer_len, inner_len = split_length(extent_y)
    first_section = mixing('kmdq,kbdeq->kmeb', spectrum, inner_table(outer_len, inner_len, 1.0)).astype(jnp.bfloat16)
    second_section = mixing('kmeb,eack->cmab', first_section, outer_table(outer_len, 1.0))
    return second_section.reshape(2, rows, extent_y)

def wave_numbers(indices, extent):
    signed = jnp.where(indices < extent // 2, indices, indices - extent)
    return signed.astype(jnp.float32) * (2.0 * math.pi / (extent * grid_step))

def propagator(angular, k_start, k_count, extent_x, extent_y):
    outer_x, inner_x = split_length(extent_x)
    outer_y, inner_y = split_length(extent_y)
    cross_ids = jnp.arange(outer_x, dtype=jnp.int32)[:, None] + outer_x * jnp.arange(inner_x, dtype=jnp.int32)[None, :]
    line_ids = (k_start + jnp.arange(k_count, dtype=jnp.int32))[:, None] + outer_y * jnp.arange(inner_y, dtype=jnp.int32)[None, :]
    wave_x = wave_numbers(cross_ids, extent_x)
    wave_y = wave_numbers(line_ids, extent_y)
    vertical = (angular * slow_ref) ** 2 - wave_x[:, None, None, :] ** 2 - wave_y[None, :, :, None] ** 2
    root_abs = jnp.sqrt(jnp.abs(vertical))
    real_part = jnp.where(vertical > 0, jnp.cos(root_abs * depth_step), jnp.exp(-root_abs * depth_step))
    imag_part = jnp.where(vertical > 0, jnp.sin(root_abs * depth_step), jnp.zeros_like(root_abs))
    return (real_part, imag_part)

def shift_phase(kspace, prop_re, prop_im):
    real_in = kspace[:, :, :, 0, :]
    imag_in = kspace[:, :, :, 1, :]
    real_out = real_in * prop_re - imag_in * prop_im
    imag_out = real_in * prop_im + imag_in * prop_re
    return jnp.stack([real_out, imag_out], axis=3).astype(jnp.bfloat16)

def block_correction(turned, matrices, block_len, extent_y):
    block_count = matrices.shape[1]
    capacity = matrices.shape[2]
    starts = (jnp.cumsum(block_len) - block_len).astype(jnp.int32)
    offsets = jnp.arange(capacity, dtype=jnp.int32)
    source = jnp.minimum(starts[:, None] + offsets[None, :], extent_y - 1).reshape(-1).astype(jnp.int32)
    occupied = (offsets[None, :] < block_len[:, None]).reshape(-1)

    def slotted(part):
        picked = jnp.take(part.astype(jnp.float32), source, axis=1)
        picked = jnp.where(occupied[None, :], picked, jnp.zeros_like(picked))
        return picked.reshape(part.shape[0], block_count, capacity)
    slot_re = slotted(turned[0])
    slot_im = slotted(turned[1])
    mat_re = matrices[0].astype(jnp.float32)
    mat_im = matrices[1].astype(jnp.float32)

    def product(first_op, second_op):
        return jnp.einsum('rcj,cij->rci', first_op, second_op, precision=highest)
    out_re = product(slot_re, mat_re) - product(slot_im, mat_im)
    out_im = product(slot_re, mat_im) + product(slot_im, mat_re)
    cell_ids = jnp.arange(extent_y, dtype=jnp.int32)
    block_end = starts + block_len
    shift_sum = lax.optimization_barrier(jnp.sum(jnp.where(block_end[None, :] <= cell_ids[:, None], capacity - block_len[None, :], 0), axis=1))
    position = (cell_ids + shift_sum).astype(jnp.int32)
    back_re = jnp.take(out_re.reshape(out_re.shape[0], -1), position, axis=1)
    back_im = jnp.take(out_im.reshape(out_im.shape[0], -1), position, axis=1)
    return (back_re, back_im)

def image_phase(angular, shot_position, depth_index):
    offset_x = (jnp.arange(NX, dtype=jnp.int32) - shot_position[0]).astype(jnp.float32) * grid_step
    offset_y = (jnp.arange(NY, dtype=jnp.int32) - shot_position[1]).astype(jnp.float32) * grid_step
    depth_now = (depth_index + 1) * depth_step
    distance = jnp.sqrt(offset_x[:, None] ** 2 + offset_y[None, :] ** 2 + depth_now * depth_now)
    return angular * slow_ref * distance

def reference(wavefield, slowness, block_inverse, block_lengths, slab_owner, shot_position):
    outer_y, inner_y = split_length(NY)

    def one_freq(carry, inputs):
        freq_index, current = inputs
        angular = 2.0 * math.pi * (band_low + band_width * (freq_index.astype(jnp.float32) + 0.5) / FREQS)
        prop_re, prop_im = propagator(angular, 0, outer_y, NX, NY)
        image_parts = []
        for depth_index in range(STEPS):
            owner_id = slab_owner[depth_index]
            slab_now = lax.dynamic_index_in_dim(slowness, owner_id, 0, keepdims=False).astype(jnp.float32)
            matrices = lax.dynamic_index_in_dim(block_inverse, owner_id, 0, keepdims=False)
            block_len = lax.dynamic_index_in_dim(block_lengths, owner_id, 0, keepdims=False)
            spectrum = forward_lines(current)
            kspace = across_forward(spectrum)
            shifted = shift_phase(kspace, prop_re, prop_im)
            restored = across_inverse(shifted, NX)
            spatial = lines_inverse(restored, NY)
            phases = angular * depth_step * (slab_now - slow_ref)
            cos_part = jnp.cos(phases)
            sin_part = jnp.sin(phases)
            turned = ((spatial[0] * cos_part - spatial[1] * sin_part).astype(jnp.bfloat16), (spatial[0] * sin_part + spatial[1] * cos_part).astype(jnp.bfloat16))
            correction = block_correction(turned, matrices, block_len, NY)
            values_re = turned[0].astype(jnp.float32) + correction[0]
            values_im = turned[1].astype(jnp.float32) + correction[1]
            angle_img = image_phase(angular, shot_position, depth_index)
            image_parts.append((values_re * jnp.cos(angle_img) - values_im * jnp.sin(angle_img)) / math.sqrt(FREQS))
            current = jnp.stack([values_re, values_im]).astype(jnp.bfloat16)
        return (carry + jnp.stack(image_parts), None)
    start_image = jnp.zeros((STEPS, NX, NY), jnp.float32)
    image, _ = lax.scan(one_freq, start_image, (jnp.arange(FREQS, dtype=jnp.int32), wavefield))
    return image
```

```python
import functools
import math

import jax
import jax.numpy as jnp
import numpy as np
from jax import lax
from jax.experimental import pallas as pl
from jax.experimental.pallas import tpu as pltpu
from jax.sharding import Mesh, PartitionSpec as P

grid_step = 0.0125
depth_step = 0.02
slow_ref = 0.4
band_low = 5.0
band_width = 55.0

INTERPRET = False
FREQ_AXES = ("yh", "x", "z")
CUT_AXES = ("yl", "core")
RADIX = 8
BLOCK_GROUP = 4
f32 = jnp.float32
bf16 = jnp.bfloat16


def dft_tables(extent):
    base = extent // RADIX
    ids = np.arange(base)
    angle = 2.0 * np.pi / base * ((ids[:, None] * ids[None, :]) % base)
    cosine = np.cos(angle) / math.sqrt(base)
    sine = np.sin(angle) / math.sqrt(base)
    forward = np.block([[cosine, sine], [-sine, cosine]])
    inverse = np.block([[cosine, -sine], [sine, cosine]])
    twist = 2.0 * np.pi / extent * (np.arange(RADIX)[:, None] * ids[None, :])
    turn = np.stack([np.cos(twist), np.sin(twist)], axis=1) / math.sqrt(RADIX)
    turn = turn.reshape(2 * RADIX, base).astype(np.float32)
    return (
        jnp.asarray(forward, bf16),
        jnp.asarray(inverse, bf16),
        jnp.asarray(turn),
        jnp.asarray(np.ascontiguousarray(turn.T)),
    )


def fft4(parts, s):
    (r0, i0), (r1, i1), (r2, i2), (r3, i3) = parts
    ar, ai, br, bi = r0 + r2, i0 + i2, r0 - r2, i0 - i2
    cr, ci, dr, di = r1 + r3, i1 + i3, r1 - r3, i1 - i3
    if s > 0:
        one, three = (br - di, bi + dr), (br + di, bi - dr)
    else:
        one, three = (br + di, bi - dr), (br - di, bi + dr)
    return [(ar + cr, ai + ci), one, (ar - cr, ai - ci), three]


def fft8(parts, s):
    even = fft4(parts[0::2], s)
    odd = fft4(parts[1::2], s)
    half = math.sqrt(0.5)
    (r0, i0), (r1, i1), (r2, i2), (r3, i3) = odd
    if s > 0:
        turned = [
            (r0, i0),
            ((r1 - i1) * half, (i1 + r1) * half),
            (-i2, r2),
            ((r3 + i3) * -half, (r3 - i3) * half),
        ]
    else:
        turned = [
            (r0, i0),
            ((r1 + i1) * half, (i1 - r1) * half),
            (i2, -r2),
            ((i3 - r3) * half, (r3 + i3) * -half),
        ]
    low = [(e[0] + t[0], e[1] + t[1]) for e, t in zip(even, turned)]
    high = [(e[0] - t[0], e[1] - t[1]) for e, t in zip(even, turned)]
    return low + high


def twist(value, cosine, sine, s):
    real, imag = value
    if s > 0:
        return (real * cosine - imag * sine, imag * cosine + real * sine)
    return (real * cosine + imag * sine, imag * cosine - real * sine)


def lines_forward_kernel(field, table, turn, out, mid):
    rows, base = out.shape[2], out.shape[3]

    def step(tile, carry):
        at = pl.ds(pl.multiple_of(tile * 16, 16), 16)
        for lane in range(0, base, 128):
            parts = []
            for a in range(RADIX):
                here = pl.ds(a * base + lane, 128)
                parts.append((field[0, at, here].astype(f32), field[1, at, here].astype(f32)))
            for k, value in enumerate(fft8(parts, -1)):
                cosine = turn[2 * k : 2 * k + 1, lane : lane + 128]
                sine = turn[2 * k + 1 : 2 * k + 2, lane : lane + 128]
                real, imag = twist(value, cosine, sine, -1)
                mid[k, at, pl.ds(lane, 128)] = real.astype(bf16)
                mid[k, at, pl.ds(base + lane, 128)] = imag.astype(bf16)
        return carry

    lax.fori_loop(0, rows // 16, step, 0)
    for k in range(RADIX):
        both = jnp.dot(mid[k], table[...], preferred_element_type=f32)
        out[k, 0] = both[:, :base].astype(bf16)
        out[k, 1] = both[:, base:].astype(bf16)


def across_kernel(field, prop_re, prop_im, forward, inverse, turn, out, mid, back):
    base, cols = prop_re.shape[1], prop_re.shape[2]

    def fore(tile, carry):
        at = pl.multiple_of(tile * 16, 16)
        for lane in range(0, cols, 128):
            here = pl.ds(lane, 128)
            parts = []
            for a in range(RADIX):
                parts.append(
                    (
                        field[a, pl.ds(at, 16), here].astype(f32),
                        field[a, pl.ds(base + at, 16), here].astype(f32),
                    )
                )
            for k, value in enumerate(fft8(parts, -1)):
                cosine = turn[pl.ds(at, 16), 2 * k : 2 * k + 1]
                sine = turn[pl.ds(at, 16), 2 * k + 1 : 2 * k + 2]
                real, imag = twist(value, cosine, sine, -1)
                mid[k, pl.ds(at, 16), here] = real.astype(bf16)
                mid[k, pl.ds(base + at, 16), here] = imag.astype(bf16)
        return carry

    lax.fori_loop(0, base // 16, fore, 0)
    for k in range(RADIX):
        both = jnp.dot(forward[...], mid[k], preferred_element_type=f32)
        real, imag = both[:base], both[base:]
        p_re, p_im = prop_re[k], prop_im[k]
        mid[k, :base] = (real * p_re - imag * p_im).astype(bf16)
        mid[k, base:] = (real * p_im + imag * p_re).astype(bf16)
        back[k] = jnp.dot(inverse[...], mid[k], preferred_element_type=f32)

    def aft(tile, carry):
        at = pl.multiple_of(tile * 16, 16)
        for lane in range(0, cols, 128):
            here = pl.ds(lane, 128)
            parts = []
            for k in range(RADIX):
                cosine = turn[pl.ds(at, 16), 2 * k : 2 * k + 1]
                sine = turn[pl.ds(at, 16), 2 * k + 1 : 2 * k + 2]
                value = (back[k, pl.ds(at, 16), here], back[k, pl.ds(base + at, 16), here])
                parts.append(twist(value, cosine, sine, 1))
            for a, (real, imag) in enumerate(fft8(parts, 1)):
                out[a, pl.ds(at, 16), here] = real.astype(bf16)
                out[a, pl.ds(base + at, 16), here] = imag.astype(bf16)
        return carry

    lax.fori_loop(0, base // 16, aft, 0)


def lines_inverse_kernel(
    windows, field, cos_u, sin_u, cos_r, sin_r, pairs, table, turn, out, back, turned, final
):
    rows, base = field.shape[2], field.shape[3]
    blocks, reach = pairs.shape[0], pairs.shape[1] // 2
    tail = pl.ds(RADIX * base, turned.shape[1] - RADIX * base)
    turned[:, tail, :] = jnp.zeros((2, tail.size, rows), bf16)
    for k in range(RADIX):
        first = lax.dot_general(
            table[:, :base], field[k, 0], (((1,), (1,)), ((), ())), preferred_element_type=f32
        )
        second = lax.dot_general(
            table[:, base:], field[k, 1], (((1,), (1,)), ((), ())), preferred_element_type=f32
        )
        back[k] = first + second

    def aft(tile, carry):
        at = pl.multiple_of(tile * 16, 16)
        for lane in range(0, rows, 128):
            here = pl.ds(lane, 128)
            parts = []
            for k in range(RADIX):
                cosine = turn[pl.ds(at, 16), 2 * k : 2 * k + 1]
                sine = turn[pl.ds(at, 16), 2 * k + 1 : 2 * k + 2]
                value = (back[k, pl.ds(at, 16), here], back[k, pl.ds(base + at, 16), here])
                parts.append(twist(value, cosine, sine, 1))
            for a, (real, imag) in enumerate(fft8(parts, 1)):
                cell = pl.ds(a * base + at, 16)
                cosine, sine = cos_u[cell, here], sin_u[cell, here]
                u_re = (real * cosine - imag * sine).astype(bf16)
                u_im = (real * sine + imag * cosine).astype(bf16)
                turned[0, cell, here] = u_re
                turned[1, cell, here] = u_im
                final[0, cell, here] = u_re.astype(f32)
                final[1, cell, here] = u_im.astype(f32)
        return carry

    lax.fori_loop(0, base // 16, aft, 0)

    def some_blocks(group, carry):
        cells, changes = [], []
        for one in range(BLOCK_GROUP):
            c = group * BLOCK_GROUP + one
            cell = pl.ds(pl.multiple_of(windows[c] * 16, 16), reach)
            both = jnp.concatenate([turned[0, cell, :], turned[1, cell, :]], axis=0)
            cells.append(cell)
            changes.append(jnp.dot(pairs[c], both, preferred_element_type=f32))
        for cell, change in zip(cells, changes):
            final[0, cell, :] += change[:reach]
            final[1, cell, :] += change[reach:]
        return carry

    lax.fori_loop(0, blocks // BLOCK_GROUP, some_blocks, 0)

    def image(tile, carry):
        cell = pl.ds(pl.multiple_of(tile * 16, 16), 16)
        across, along, high, piece = out.shape[:4]
        owner, place = tile * 16 // piece, tile * 16 % piece
        spot = pl.ds(pl.multiple_of(place, 16), 16)
        out[owner // along % across, owner % along, owner // (along * across), spot, :] = (
            final[0, cell, :] * cos_r[cell, :] - final[1, cell, :] * sin_r[cell, :]
        ).astype(bf16)
        return carry

    lax.fori_loop(0, RADIX * base // 16, image, 0)


def call(kernel, out_shape, scratch, *operands, scalars=0):
    smem = pl.BlockSpec(memory_space=pltpu.SMEM)
    vmem = pl.BlockSpec(memory_space=pltpu.VMEM)
    return pl.pallas_call(
        kernel,
        out_shape=out_shape,
        in_specs=[smem] * scalars + [vmem] * (len(operands) - scalars),
        out_specs=vmem,
        scratch_shapes=scratch,
        interpret=INTERPRET,
    )(*operands)


def wave_numbers(indices, extent):
    signed = jnp.where(indices < extent // 2, indices, indices - extent)
    return signed.astype(f32) * (2.0 * math.pi / (extent * grid_step))


def propagator(angular, cut_index, extent_x, extent_y):
    cross_ids = (
        jnp.arange(RADIX, dtype=jnp.int32)[:, None]
        + RADIX * jnp.arange(extent_x // RADIX, dtype=jnp.int32)[None, :]
    )
    line_ids = cut_index + RADIX * jnp.arange(extent_y // RADIX, dtype=jnp.int32)
    wave_x = wave_numbers(cross_ids, extent_x)
    wave_y = wave_numbers(line_ids, extent_y)
    vertical = (angular * slow_ref) ** 2 - wave_x[:, :, None] ** 2 - wave_y[None, None, :] ** 2
    root_abs = jnp.sqrt(jnp.abs(vertical))
    real_part = jnp.where(
        vertical > 0, jnp.cos(root_abs * depth_step), jnp.exp(-root_abs * depth_step)
    )
    imag_part = jnp.where(vertical > 0, jnp.sin(root_abs * depth_step), jnp.zeros_like(root_abs))
    return (real_part, imag_part)


def rotations(size):
    return [[(i, (i + d) % size) for i in range(size)] for d in range(1, size)]


def split_ring(value, axis, owner):
    size = lax.axis_size(axis)
    me = lax.axis_index(axis)
    shaped = value.reshape((size, value.shape[0] // size) + value.shape[1:])
    piece = lax.dynamic_index_in_dim(shaped, me, 0, keepdims=False)
    for d, pairs in enumerate(rotations(size), 1):
        sent = lax.dynamic_index_in_dim(shaped, (me + d) % size, 0, keepdims=False)
        got = lax.ppermute(sent, axis, pairs)
        piece = jnp.where((me - owner) % size == d, got, piece)
    return piece


def join_ring(piece, axis):
    size = lax.axis_size(axis)
    me = lax.axis_index(axis)
    out = jnp.zeros((size,) + piece.shape, piece.dtype)
    out = lax.dynamic_update_index_in_dim(out, piece, me, 0)
    for d, pairs in enumerate(rotations(size), 1):
        got = lax.ppermute(piece, axis, pairs)
        out = lax.dynamic_update_index_in_dim(out, got, (me - d) % size, 0)
    return out.reshape((-1,) + piece.shape[1:])


def swap(value, axis, bit):
    return lax.ppermute(value, axis, [(i, i ^ bit) for i in range(lax.axis_size(axis))])


def bits_of(size):
    return [1 << i for i in range(size.bit_length() - 1)]


def split_hops(value, axis, owner):
    me = lax.axis_index(axis)
    for bit in bits_of(lax.axis_size(axis)):
        mine = (me & bit) != 0
        half = value.shape[0] // 2
        low, high = value[:half], value[half:]
        got = swap(jnp.where(mine, low, high), axis, bit)
        value = jnp.where(((owner ^ me) & bit) == 0, jnp.where(mine, high, low), got)
    return value


def join_hops(piece, axis, bits=None):
    me = lax.axis_index(axis)
    for bit in bits_of(lax.axis_size(axis))[::-1] if bits is None else bits:
        mine = (me & bit) != 0
        got = swap(piece, axis, bit)
        piece = jnp.concatenate([jnp.where(mine, got, piece), jnp.where(mine, piece, got)], axis=0)
    return piece


def from_owner(value, owner_id):
    across, along = lax.axis_size("x"), lax.axis_size("z")
    piece = split_ring(value, "x", owner_id // along % across)
    piece = split_hops(piece, "z", owner_id % along)
    if lax.axis_size("yh") > 1:
        other = swap(piece, "yh", 1)
        same = lax.axis_index("yh") == owner_id // (across * along)
        piece = jnp.where(same, piece, other)
    return piece


def sum_over(part, axis, kind):
    terms = lax.all_to_all(part, axis, 0, 0)
    return jnp.sum(terms.astype(f32), axis=0).astype(kind)


def block_windows(matrices, starts, lengths):
    capacity = matrices.shape[2]
    reach = capacity + 16
    windows = starts // 16
    slots = jnp.arange(capacity, dtype=jnp.int32)
    spots = jnp.arange(reach, dtype=jnp.int32)
    place = (spots[None, :, None] == slots[None, None, :] + (starts % 16)[:, None, None]) & (
        slots[None, None, :] < lengths[:, None, None]
    )
    place = place.astype(bf16)
    moved = jnp.einsum("cia,dcab->dcib", place, matrices, preferred_element_type=f32).astype(bf16)
    moved = jnp.einsum("dcib,cjb->dcij", moved, place, preferred_element_type=f32).astype(bf16)
    upper = jnp.concatenate([moved[0], -moved[1]], axis=2)
    lower = jnp.concatenate([moved[1], moved[0]], axis=2)
    return windows, jnp.concatenate([upper, lower], axis=1)


def body(wavefield, slowness, block_inverse, block_lengths, slab_owner, shot_position):
    counts = tuple(lax.axis_size(name) for name in FREQ_AXES)
    freq_total = math.prod(counts)
    cut_count = lax.axis_size("yl") * lax.axis_size("core")
    row_count, extent_y = wavefield.shape[2], wavefield.shape[3]
    extent_x = row_count * cut_count
    base = extent_y // RADIX
    freq_index = lax.axis_index(FREQ_AXES)
    cut_index = lax.axis_index(CUT_AXES)
    angular = (
        2.0 * math.pi * (band_low + band_width * (freq_index.astype(f32) + 0.5) / freq_total)
    )
    forward, inverse, turn_rows, turn_cols = dft_tables(extent_y)

    spectrum = call(
        lines_forward_kernel,
        jax.ShapeDtypeStruct((RADIX, 2, row_count, base), bf16),
        [pltpu.VMEM((RADIX, row_count, 2 * base), bf16)],
        wavefield[0], inverse, turn_rows,
    )
    spectrum, slowness, block_inverse = lax.optimization_barrier(
        (spectrum, slowness, block_inverse)
    )
    columns = lax.all_to_all(
        spectrum.reshape(RADIX, 2 * row_count, base), CUT_AXES, 0, 0, tiled=True
    )
    prop_re, prop_im = propagator(angular, cut_index, extent_x, extent_y)

    owner_id = slab_owner[0]
    with jax.named_scope("spread"):
        pieces = counts[1] * counts[2] * 16
        joined = jnp.concatenate(
            [slowness[0].T, block_inverse[0].reshape(-1, row_count)], axis=0
        )
        filled = joined.shape[0]
        joined = jnp.pad(joined, ((0, -filled % pieces), (0, 0)))
        share = from_owner(joined, owner_id)
        along_bits = bits_of(counts[2])[::-1]
        share = join_hops(share, "z", along_bits[:2])
        columns, prop_re, prop_im, share = lax.optimization_barrier(
            (columns, prop_re, prop_im, share)
        )
        share = join_hops(share, "z", along_bits[2:])
        joined = join_ring(share, "x")
        slab = joined[:extent_y]
        operators = join_hops(joined[extent_y:filled], "core")
        operators = join_ring(operators, "yl")
    shape = block_inverse.shape
    matrices = operators.reshape((cut_count,) + shape[1:]).transpose(1, 0, 2, 3, 4)
    matrices = matrices.reshape(2, -1, shape[3], shape[4])
    lengths = lax.dynamic_index_in_dim(block_lengths, owner_id, 0, keepdims=False)
    starts = jnp.cumsum(lengths) - lengths
    windows, pairs = block_windows(matrices, starts, lengths)
    phases = angular * depth_step * (slab.astype(f32) - slow_ref)
    cos_u, sin_u = jnp.cos(phases), jnp.sin(phases)

    rows_x = cut_index * row_count + jnp.arange(row_count, dtype=jnp.int32)
    offset_x = (rows_x - shot_position[0]).astype(f32) * grid_step
    offset_y = (jnp.arange(extent_y, dtype=jnp.int32) - shot_position[1]).astype(f32) * grid_step
    distance = jnp.sqrt(
        offset_x[None, :] ** 2 + offset_y[:, None] ** 2 + depth_step * depth_step
    )
    ray = angular * slow_ref * distance
    level = 1.0 / math.sqrt(freq_total)
    cos_r, sin_r = jnp.cos(ray) * level, jnp.sin(ray) * level

    restored = call(
        across_kernel,
        jax.ShapeDtypeStruct((RADIX, 2 * row_count, base), bf16),
        [
            pltpu.VMEM((RADIX, 2 * row_count, base), bf16),
            pltpu.VMEM((RADIX, 2 * row_count, base), f32),
        ],
        columns, prop_re, prop_im, forward, inverse, turn_cols,
    )
    row_field = lax.all_to_all(restored, CUT_AXES, 0, 0, tiled=True)
    capacity = block_inverse.shape[3]
    part = call(
        lines_inverse_kernel,
        jax.ShapeDtypeStruct(
            counts[1:] + (counts[0], extent_y // freq_total, row_count), bf16
        ),
        [
            pltpu.VMEM((RADIX, 2 * base, row_count), f32),
            pltpu.VMEM((2, extent_y + capacity, row_count), bf16),
            pltpu.VMEM((2, extent_y + capacity, row_count), f32),
        ],
        windows, row_field.reshape(RADIX, 2, row_count, base),
        cos_u, sin_u, cos_r, sin_r, pairs, inverse, turn_cols,
        scalars=1,
    )
    part = sum_over(part, "x", bf16)
    part = sum_over(part, "z", bf16)
    image = sum_over(part, "yh", f32)
    return image.T[None]


def solution(mesh):
    sizes = {"yh": 2, "x": 4, "z": 8, "yl": 4, "core": 2}
    if mesh.devices.size != math.prod(sizes.values()):
        sizes = {"yh": 1, "x": 1, "z": 1, "yl": 4, "core": 2}
    fine = Mesh(mesh.devices.reshape(tuple(sizes.values())), tuple(sizes))
    placed = (
        P(FREQ_AXES, None, CUT_AXES, None),
        P(FREQ_AXES, CUT_AXES, None),
        P(FREQ_AXES, None, CUT_AXES, None, None),
        P(),
        P(),
        P(),
    )
    return jax.shard_map(
        body, mesh=fine, in_specs=placed, out_specs=P(None, CUT_AXES, FREQ_AXES), check_vma=False
    )
```

```python
import math

import jax
import jax.numpy as jnp
import numpy as np
from jax import lax
from jax.experimental import pallas as pl
from jax.experimental.pallas import tpu as pltpu
from jax.sharding import Mesh, PartitionSpec as P

grid_step = 0.0125
depth_step = 0.02
slow_ref = 0.4
band_low = 5.0
band_width = 55.0

INTERPRET = False
FREQ_AXES = ("yh", "x", "z")
CUT_AXES = ("yl", "core")
RADIX = 8
BLOCK_GROUP = 4
f32 = jnp.float32
bf16 = jnp.bfloat16


def dft_tables(extent):
    base = extent // RADIX
    ids = np.arange(base)
    angle = 2.0 * np.pi / base * ((ids[:, None] * ids[None, :]) % base)
    cosine = np.cos(angle) / math.sqrt(base)
    sine = np.sin(angle) / math.sqrt(base)
    inverse = np.block([[cosine, -sine], [sine, cosine]])
    twists = 2.0 * np.pi / extent * (np.arange(RADIX)[:, None] * np.arange(extent)[None, :])
    turn = np.stack([np.cos(twists), np.sin(twists)], axis=1) / math.sqrt(RADIX)
    turn = turn.reshape(2 * RADIX, extent).astype(np.float32)
    return jnp.asarray(inverse, bf16), jnp.asarray(turn)


def fft4(parts, s):
    (r0, i0), (r1, i1), (r2, i2), (r3, i3) = parts
    ar, ai, br, bi = r0 + r2, i0 + i2, r0 - r2, i0 - i2
    cr, ci, dr, di = r1 + r3, i1 + i3, r1 - r3, i1 - i3
    if s > 0:
        one, three = (br - di, bi + dr), (br + di, bi - dr)
    else:
        one, three = (br + di, bi - dr), (br - di, bi + dr)
    return [(ar + cr, ai + ci), one, (ar - cr, ai - ci), three]


def fft8(parts, s):
    even = fft4(parts[0::2], s)
    odd = fft4(parts[1::2], s)
    half = math.sqrt(0.5)
    (r0, i0), (r1, i1), (r2, i2), (r3, i3) = odd
    if s > 0:
        turned = [
            (r0, i0),
            ((r1 - i1) * half, (i1 + r1) * half),
            (-i2, r2),
            ((r3 + i3) * -half, (r3 - i3) * half),
        ]
    else:
        turned = [
            (r0, i0),
            ((r1 + i1) * half, (i1 - r1) * half),
            (i2, -r2),
            ((i3 - r3) * half, (r3 + i3) * -half),
        ]
    low = [(e[0] + t[0], e[1] + t[1]) for e, t in zip(even, turned)]
    high = [(e[0] - t[0], e[1] - t[1]) for e, t in zip(even, turned)]
    return low + high


def twist(value, cosine, sine, s):
    real, imag = value
    if s > 0:
        return (real * cosine - imag * sine, imag * cosine + real * sine)
    return (real * cosine + imag * sine, imag * cosine - real * sine)


def lines_forward_kernel(me, field, table, turn, *outs_mid):
    outs, mid = outs_mid[:RADIX], outs_mid[RADIX]
    rows, base = mid.shape[1], mid.shape[2] // 2

    def step(tile, carry):
        at = pl.ds(pl.multiple_of(tile * 16, 16), 16)
        for lane in range(0, base, 128):
            parts = []
            for a in range(RADIX):
                here = pl.ds(a * base + lane, 128)
                parts.append((field[0, at, here].astype(f32), field[1, at, here].astype(f32)))
            for k, value in enumerate(fft8(parts, -1)):
                cosine = turn[2 * k : 2 * k + 1, lane : lane + 128]
                sine = turn[2 * k + 1 : 2 * k + 2, lane : lane + 128]
                real, imag = twist(value, cosine, sine, -1)
                mid[k, at, pl.ds(lane, 128)] = real.astype(bf16)
                mid[k, at, pl.ds(base + lane, 128)] = imag.astype(bf16)
        return carry

    lax.fori_loop(0, rows // 16, step, 0)
    for d, out in enumerate(outs):
        both = jnp.dot(mid[(me[0] + d) % RADIX], table[...], preferred_element_type=f32)
        out[:rows] = both[:, :base].astype(bf16)
        out[rows:] = both[:, base:].astype(bf16)


def across_kernel(*refs):
    fields, refs = refs[:RADIX], refs[RADIX:]
    prop_re, prop_im, table, turn = refs[:4]
    outs, (mid, back) = refs[4 : 4 + RADIX], refs[4 + RADIX :]
    base, cols = prop_re.shape[1], prop_re.shape[2]

    def fore(tile, carry):
        at = pl.multiple_of(tile * 16, 16)
        for lane in range(0, cols, 128):
            here = pl.ds(lane, 128)
            parts = []
            for field in fields:
                parts.append(
                    (
                        field[pl.ds(at, 16), here].astype(f32),
                        field[pl.ds(base + at, 16), here].astype(f32),
                    )
                )
            for k, value in enumerate(fft8(parts, 1)):
                cosine = turn[pl.ds(at, 16), 2 * k : 2 * k + 1]
                sine = turn[pl.ds(at, 16), 2 * k + 1 : 2 * k + 2]
                real, imag = twist(value, cosine, sine, -1)
                mid[k, pl.ds(at, 16), here] = real.astype(bf16)
                mid[k, pl.ds(base + at, 16), here] = (-imag).astype(bf16)
        return carry

    lax.fori_loop(0, base // 16, fore, 0)
    for k in range(RADIX):
        both = jnp.dot(table[...], mid[k], preferred_element_type=f32)
        real, minus = both[:base], both[base:]
        p_re, p_im = prop_re[k], prop_im[k]
        mid[k, :base] = (real * p_re + minus * p_im).astype(bf16)
        mid[k, base:] = (real * p_im - minus * p_re).astype(bf16)
        back[k] = jnp.dot(table[...], mid[k], preferred_element_type=f32)

    def aft(tile, carry):
        at = pl.multiple_of(tile * 16, 16)
        for lane in range(0, cols, 128):
            here = pl.ds(lane, 128)
            parts = []
            for k in range(RADIX):
                cosine = turn[pl.ds(at, 16), 2 * k : 2 * k + 1]
                sine = turn[pl.ds(at, 16), 2 * k + 1 : 2 * k + 2]
                value = (back[k, pl.ds(at, 16), here], back[k, pl.ds(base + at, 16), here])
                parts.append(twist(value, cosine, sine, 1))
            for out, (real, imag) in zip(outs, fft8(parts, 1)):
                out[pl.ds(at, 16), here] = real.astype(bf16)
                out[pl.ds(base + at, 16), here] = imag.astype(bf16)
        return carry

    lax.fori_loop(0, base // 16, aft, 0)


def lines_inverse_kernel(me, windows, *refs):
    fields, refs = refs[:RADIX], refs[RADIX:]
    cos_u, sin_u, cos_r, sin_r, pairs, table, turn, out, back, turned, final = refs
    rows, base = fields[0].shape[0] // 2, fields[0].shape[1]
    blocks, reach = pairs.shape[0], pairs.shape[1] // 2
    tail = pl.ds(RADIX * base, turned.shape[1] - RADIX * base)
    turned[:, tail, :] = jnp.zeros((2, tail.size, rows), bf16)
    for d, field in enumerate(fields):
        first = lax.dot_general(
            table[:, :base], field[:rows], (((1,), (1,)), ((), ())), preferred_element_type=f32
        )
        second = lax.dot_general(
            table[:, base:], field[rows:], (((1,), (1,)), ((), ())), preferred_element_type=f32
        )
        back[(me[0] + RADIX - d) % RADIX] = first + second

    def aft(tile, carry):
        at = pl.multiple_of(tile * 16, 16)
        for lane in range(0, rows, 128):
            here = pl.ds(lane, 128)
            parts = []
            for k in range(RADIX):
                cosine = turn[pl.ds(at, 16), 2 * k : 2 * k + 1]
                sine = turn[pl.ds(at, 16), 2 * k + 1 : 2 * k + 2]
                value = (back[k, pl.ds(at, 16), here], back[k, pl.ds(base + at, 16), here])
                parts.append(twist(value, cosine, sine, 1))
            for a, (real, imag) in enumerate(fft8(parts, 1)):
                cell = pl.ds(a * base + at, 16)
                cosine, sine = cos_u[cell, here], sin_u[cell, here]
                u_re = (real * cosine - imag * sine).astype(bf16)
                u_im = (real * sine + imag * cosine).astype(bf16)
                turned[0, cell, here] = u_re
                turned[1, cell, here] = u_im
                final[0, cell, here] = u_re.astype(f32)
                final[1, cell, here] = u_im.astype(f32)
        return carry

    lax.fori_loop(0, base // 16, aft, 0)

    def some_blocks(group, carry):
        cells, changes = [], []
        for one in range(BLOCK_GROUP):
            c = group * BLOCK_GROUP + one
            cell = pl.ds(pl.multiple_of(windows[c] * 16, 16), reach)
            both = jnp.concatenate([turned[0, cell, :], turned[1, cell, :]], axis=0)
            cells.append(cell)
            changes.append(jnp.dot(pairs[c], both, preferred_element_type=f32))
        for cell, change in zip(cells, changes):
            final[0, cell, :] += change[:reach]
            final[1, cell, :] += change[reach:]
        return carry

    lax.fori_loop(0, blocks // BLOCK_GROUP, some_blocks, 0)

    def image(tile, carry):
        cell = pl.ds(pl.multiple_of(tile * 16, 16), 16)
        across, _, along, piece = out.shape[:4]
        owner, place = tile * 16 // piece, tile * 16 % piece
        spot = pl.ds(pl.multiple_of(place, 16), 16)
        out[owner // along % across, owner // (along * across), owner % along, spot, :] = (
            final[0, cell, :] * cos_r[cell, :] - final[1, cell, :] * sin_r[cell, :]
        ).astype(bf16)
        return carry

    lax.fori_loop(0, RADIX * base // 16, image, 0)


def call(kernel, out_shape, scratch, *operands, scalars=0):
    smem = pl.BlockSpec(memory_space=pltpu.SMEM)
    vmem = pl.BlockSpec(memory_space=pltpu.VMEM)
    return pl.pallas_call(
        kernel,
        out_shape=out_shape,
        in_specs=[smem] * scalars + [vmem] * (len(operands) - scalars),
        out_specs=jax.tree.map(lambda _: vmem, out_shape),
        scratch_shapes=scratch,
        interpret=INTERPRET,
    )(*operands)


def wave_numbers(indices, extent):
    signed = jnp.where(indices < extent // 2, indices, indices - extent)
    return signed.astype(f32) * (2.0 * math.pi / (extent * grid_step))


def propagator(angular, cut_index, extent_x, extent_y):
    cross_ids = (
        jnp.arange(RADIX, dtype=jnp.int32)[:, None]
        + RADIX * jnp.arange(extent_x // RADIX, dtype=jnp.int32)[None, :]
    )
    line_ids = cut_index + RADIX * jnp.arange(extent_y // RADIX, dtype=jnp.int32)
    wave_x = wave_numbers(cross_ids, extent_x)
    wave_y = wave_numbers(line_ids, extent_y)
    vertical = (angular * slow_ref) ** 2 - wave_x[:, :, None] ** 2 - wave_y[None, None, :] ** 2
    root_abs = jnp.sqrt(jnp.abs(vertical))
    real_part = jnp.where(
        vertical > 0, jnp.cos(root_abs * depth_step), jnp.exp(-root_abs * depth_step)
    )
    imag_part = jnp.where(vertical > 0, jnp.sin(root_abs * depth_step), jnp.zeros_like(root_abs))
    return (real_part, imag_part)


def rotate(values, axes):
    size = math.prod(lax.axis_size(axis) for axis in axes)
    got = [values[0]]
    for d in range(1, size):
        got.append(lax.ppermute(values[d], axes, [(i, (i + d) % size) for i in range(size)]))
    return got


def split(value, axis, owner):
    size = lax.axis_size(axis)
    shaped = value.reshape((size, value.shape[0] // size) + value.shape[1:])
    shaped = lax.all_to_all(shaped, axis, 0, 0)
    return lax.dynamic_index_in_dim(shaped, owner, 0, keepdims=False)


def join(piece, axis):
    copies = jnp.broadcast_to(piece[None], (lax.axis_size(axis),) + piece.shape)
    copies = lax.all_to_all(copies, axis, 0, 0)
    return copies.reshape((-1,) + piece.shape[1:])


def swap(value, axis, bit):
    return lax.ppermute(value, axis, [(i, i ^ bit) for i in range(lax.axis_size(axis))])


def from_owner(value, owner_id):
    across, along = lax.axis_size("x"), lax.axis_size("z")
    piece = split(value, "x", owner_id // along % across)
    piece = split(piece, "z", owner_id % along)
    if lax.axis_size("yh") > 1:
        other = swap(piece, "yh", 1)
        same = lax.axis_index("yh") == owner_id // (across * along)
        piece = jnp.where(same, piece, other)
    return piece


def sum_over(part, axis, kind):
    terms = lax.all_to_all(part, axis, 0, 0, tiled=True)
    return jnp.sum(terms.astype(f32), axis=0).astype(kind)


def block_windows(matrices, starts, lengths):
    capacity = matrices.shape[2]
    reach = capacity + 16
    windows = starts // 16
    slots = jnp.arange(capacity, dtype=jnp.int32)
    spots = jnp.arange(reach, dtype=jnp.int32)
    place = (spots[None, :, None] == slots[None, None, :] + (starts % 16)[:, None, None]) & (
        slots[None, None, :] < lengths[:, None, None]
    )
    place = place.astype(bf16)
    moved = jnp.einsum("cia,dcab->dcib", place, matrices, preferred_element_type=f32).astype(bf16)
    moved = jnp.einsum("dcib,cjb->dcij", moved, place, preferred_element_type=f32).astype(bf16)
    upper = jnp.concatenate([moved[0], -moved[1]], axis=2)
    lower = jnp.concatenate([moved[1], moved[0]], axis=2)
    return windows, jnp.concatenate([upper, lower], axis=1)


def step(wavefield, slowness, block_inverse, block_lengths, slab_owner, shot_position):
    counts = tuple(lax.axis_size(name) for name in FREQ_AXES)
    freq_total = math.prod(counts)
    cut_count = lax.axis_size("yl") * lax.axis_size("core")
    row_count, extent_y = wavefield.shape[2], wavefield.shape[3]
    extent_x = row_count * cut_count
    base = extent_y // RADIX
    freq_index = lax.axis_index(FREQ_AXES)
    cut_index = lax.axis_index(CUT_AXES)
    device = cut_index.reshape(1).astype(jnp.int32)
    angular = (
        2.0 * math.pi * (band_low + band_width * (freq_index.astype(f32) + 0.5) / freq_total)
    )
    inverse, turn = dft_tables(extent_y)
    turn_rows = turn[:, :base]
    turn_here = lax.dynamic_slice_in_dim(turn, cut_index * base, base, 1).T
    turn_cols = turn_rows.T
    chunk = jax.ShapeDtypeStruct((2 * row_count, base), bf16)

    spectrum = call(
        lines_forward_kernel,
        [chunk] * RADIX,
        [pltpu.VMEM((RADIX, row_count, 2 * base), bf16)],
        device, wavefield[0], inverse, turn_rows,
        scalars=1,
    )
    spectrum, slowness, block_inverse = lax.optimization_barrier(
        (spectrum, slowness, block_inverse)
    )
    columns = rotate(spectrum, CUT_AXES)

    prop_re, prop_im = propagator(angular, cut_index, extent_x, extent_y)
    rows_x = cut_index * row_count + jnp.arange(row_count, dtype=jnp.int32)
    offset_x = (rows_x - shot_position[0]).astype(f32) * grid_step
    offset_y = (jnp.arange(extent_y, dtype=jnp.int32) - shot_position[1]).astype(f32) * grid_step
    distance = jnp.sqrt(
        offset_x[None, :] ** 2 + offset_y[:, None] ** 2 + depth_step * depth_step
    )
    ray = angular * slow_ref * distance
    level = 1.0 / math.sqrt(freq_total)
    cos_r, sin_r = jnp.cos(ray) * level, jnp.sin(ray) * level
    owner_id = slab_owner[0]
    pieces = counts[1] * counts[2] * 16
    joined = jnp.concatenate([slowness[0].T, block_inverse[0].reshape(-1, row_count)], axis=0)
    filled = joined.shape[0]
    joined = jnp.pad(joined, ((0, -filled % pieces), (0, 0)))
    share = join(from_owner(joined, owner_id), "z")
    columns, prop_re, prop_im, cos_r, sin_r, share = lax.optimization_barrier(
        (columns, prop_re, prop_im, cos_r, sin_r, share)
    )

    restored = call(
        across_kernel,
        [chunk] * RADIX,
        [
            pltpu.VMEM((RADIX, 2 * row_count, base), bf16),
            pltpu.VMEM((RADIX, 2 * row_count, base), f32),
        ],
        *columns, prop_re, prop_im, inverse, turn_here,
    )
    row_field = rotate(restored, CUT_AXES)

    joined, _ = lax.optimization_barrier((join(share, "x"), restored[0]))
    mine = joined[extent_y:filled]
    other = swap(mine, "core", 1)
    first = lax.axis_index("core") == 0
    operators = jnp.concatenate(
        [jnp.where(first, mine, other), jnp.where(first, other, mine)], axis=0
    )
    operators = join(operators, "yl")
    shape = block_inverse.shape
    matrices = operators.reshape((cut_count,) + shape[1:]).transpose(1, 0, 2, 3, 4)
    matrices = matrices.reshape(2, -1, shape[3], shape[4])
    lengths = lax.dynamic_index_in_dim(block_lengths, owner_id, 0, keepdims=False)
    starts = jnp.cumsum(lengths) - lengths
    windows, pairs = block_windows(matrices, starts, lengths)
    phases = angular * depth_step * (joined[:extent_y].astype(f32) - slow_ref)
    cos_u, sin_u = jnp.cos(phases), jnp.sin(phases)

    part = call(
        lines_inverse_kernel,
        jax.ShapeDtypeStruct(
            (counts[1], counts[0], counts[2], extent_y // freq_total, row_count), bf16
        ),
        [
            pltpu.VMEM((RADIX, 2 * base, row_count), f32),
            pltpu.VMEM((2, extent_y + shape[3], row_count), bf16),
            pltpu.VMEM((2, extent_y + shape[3], row_count), f32),
        ],
        device, windows, *row_field,
        cos_u, sin_u, cos_r, sin_r, pairs, inverse, turn_cols,
        scalars=2,
    )
    part = sum_over(part, "x", bf16)
    part = part.reshape((counts[0] * counts[2],) + part.shape[2:])
    image = sum_over(part, ("yh", "z"), f32)
    return image.T[None]


def solution(mesh):
    sizes = {"yh": 2, "x": 4, "z": 8, "yl": 4, "core": 2}
    if mesh.devices.size != math.prod(sizes.values()):
        sizes = {"yh": 1, "x": 1, "z": 1, "yl": 4, "core": 2}
    fine = Mesh(mesh.devices.reshape(tuple(sizes.values())), tuple(sizes))
    placed = (
        P(FREQ_AXES, None, CUT_AXES, None),
        P(FREQ_AXES, CUT_AXES, None),
        P(FREQ_AXES, None, CUT_AXES, None, None),
        P(),
        P(),
        P(),
    )
    return jax.shard_map(
        step, mesh=fine, in_specs=placed, out_specs=P(None, CUT_AXES, FREQ_AXES), check_vma=False
    )
```

```python
import math

import jax
import jax.numpy as jnp
import numpy as np
from jax import lax
from jax.experimental import pallas as pl
from jax.experimental.pallas import tpu as pltpu
from jax.sharding import Mesh, PartitionSpec as P

grid_step = 0.0125
depth_step = 0.02
slow_ref = 0.4
band_low = 5.0
band_width = 55.0

INTERPRET = False
FREQ_AXES = ("yh", "x", "z")
CUT_AXES = ("yl", "core")
RADIX = 8
BLOCK_GROUP = 4
f32 = jnp.float32
bf16 = jnp.bfloat16


def dft_tables(extent):
    base = extent // RADIX
    ids = np.arange(base)
    angle = 2.0 * np.pi / base * ((ids[:, None] * ids[None, :]) % base)
    cosine = np.cos(angle) / math.sqrt(base)
    sine = np.sin(angle) / math.sqrt(base)
    inverse = np.block([[cosine, -sine], [sine, cosine]])
    twists = 2.0 * np.pi / extent * (np.arange(RADIX)[:, None] * np.arange(extent)[None, :])
    turn = np.stack([np.cos(twists), np.sin(twists)], axis=1) / math.sqrt(RADIX)
    turn = turn.reshape(2 * RADIX, extent).astype(np.float32)
    return jnp.asarray(inverse, bf16), jnp.asarray(turn)


def fft4(parts, s):
    (r0, i0), (r1, i1), (r2, i2), (r3, i3) = parts
    ar, ai, br, bi = r0 + r2, i0 + i2, r0 - r2, i0 - i2
    cr, ci, dr, di = r1 + r3, i1 + i3, r1 - r3, i1 - i3
    if s > 0:
        one, three = (br - di, bi + dr), (br + di, bi - dr)
    else:
        one, three = (br + di, bi - dr), (br - di, bi + dr)
    return [(ar + cr, ai + ci), one, (ar - cr, ai - ci), three]


def fft8(parts, s):
    even = fft4(parts[0::2], s)
    odd = fft4(parts[1::2], s)
    half = math.sqrt(0.5)
    (r0, i0), (r1, i1), (r2, i2), (r3, i3) = odd
    if s > 0:
        turned = [
            (r0, i0),
            ((r1 - i1) * half, (i1 + r1) * half),
            (-i2, r2),
            ((r3 + i3) * -half, (r3 - i3) * half),
        ]
    else:
        turned = [
            (r0, i0),
            ((r1 + i1) * half, (i1 - r1) * half),
            (i2, -r2),
            ((i3 - r3) * half, (r3 + i3) * -half),
        ]
    low = [(e[0] + t[0], e[1] + t[1]) for e, t in zip(even, turned)]
    high = [(e[0] - t[0], e[1] - t[1]) for e, t in zip(even, turned)]
    return low + high


def twist(value, cosine, sine, s):
    real, imag = value
    if s > 0:
        return (real * cosine - imag * sine, imag * cosine + real * sine)
    return (real * cosine + imag * sine, imag * cosine - real * sine)


def fetch(sources, targets, done):
    copies = [
        pltpu.make_async_copy(source, target, done.at[i])
        for i, (source, target) in enumerate(zip(sources, targets))
    ]
    for copy in copies:
        copy.start()
    return copies


def lines_forward_kernel(me, field, table, turn, *outs_mid):
    outs, mid = outs_mid[:RADIX], outs_mid[RADIX]
    rows, base = mid.shape[1], mid.shape[2] // 2

    def step(tile, carry):
        at = pl.ds(pl.multiple_of(tile * 16, 16), 16)
        for lane in range(0, base, 128):
            parts = []
            for a in range(RADIX):
                here = pl.ds(a * base + lane, 128)
                parts.append((field[0, at, here].astype(f32), field[1, at, here].astype(f32)))
            for k, value in enumerate(fft8(parts, -1)):
                cosine = turn[2 * k : 2 * k + 1, lane : lane + 128]
                sine = turn[2 * k + 1 : 2 * k + 2, lane : lane + 128]
                real, imag = twist(value, cosine, sine, -1)
                mid[k, at, pl.ds(lane, 128)] = real.astype(bf16)
                mid[k, at, pl.ds(base + lane, 128)] = imag.astype(bf16)
        return carry

    lax.fori_loop(0, rows // 16, step, 0)
    for d, out in enumerate(outs):
        both = jnp.dot(mid[(me[0] + d) % RADIX], table[...], preferred_element_type=f32)
        out[:rows] = both[:, :base].astype(bf16)
        out[rows:] = both[:, base:].astype(bf16)


def across_kernel(*refs):
    fields, refs = refs[:RADIX], refs[RADIX:]
    table, turn = refs[:2]
    later, refs = refs[2:4], refs[4:]
    outs, (mid, back, prop_re, prop_im, done) = refs[:RADIX], refs[RADIX:]
    copies = fetch(later, (prop_re, prop_im), done)
    base, cols = prop_re.shape[1], prop_re.shape[2]

    def fore(tile, carry):
        at = pl.multiple_of(tile * 16, 16)
        for lane in range(0, cols, 128):
            here = pl.ds(lane, 128)
            parts = []
            for field in fields:
                parts.append(
                    (
                        field[pl.ds(at, 16), here].astype(f32),
                        field[pl.ds(base + at, 16), here].astype(f32),
                    )
                )
            for k, value in enumerate(fft8(parts, 1)):
                cosine = turn[pl.ds(at, 16), 2 * k : 2 * k + 1]
                sine = turn[pl.ds(at, 16), 2 * k + 1 : 2 * k + 2]
                real, imag = twist(value, cosine, sine, -1)
                mid[k, pl.ds(at, 16), here] = real.astype(bf16)
                mid[k, pl.ds(base + at, 16), here] = (-imag).astype(bf16)
        return carry

    lax.fori_loop(0, base // 16, fore, 0)
    for copy in copies:
        copy.wait()

    def waves(step, carry):
        for k in (2 * step, 2 * step + 1):
            both = jnp.dot(table[...], mid[k], preferred_element_type=f32)
            real, minus = both[:base], both[base:]
            p_re, p_im = prop_re[k], prop_im[k]
            mid[k, :base] = (real * p_re + minus * p_im).astype(bf16)
            mid[k, base:] = (real * p_im - minus * p_re).astype(bf16)
            back[k] = jnp.dot(table[...], mid[k], preferred_element_type=f32)
        return carry

    lax.fori_loop(0, RADIX // 2, waves, 0)

    def aft(tile, carry):
        at = pl.multiple_of(tile * 16, 16)
        for lane in range(0, cols, 128):
            here = pl.ds(lane, 128)
            parts = []
            for k in range(RADIX):
                cosine = turn[pl.ds(at, 16), 2 * k : 2 * k + 1]
                sine = turn[pl.ds(at, 16), 2 * k + 1 : 2 * k + 2]
                value = (back[k, pl.ds(at, 16), here], back[k, pl.ds(base + at, 16), here])
                parts.append(twist(value, cosine, sine, 1))
            for out, (real, imag) in zip(outs, fft8(parts, 1)):
                out[pl.ds(at, 16), here] = real.astype(bf16)
                out[pl.ds(base + at, 16), here] = imag.astype(bf16)
        return carry

    lax.fori_loop(0, base // 16, aft, 0)


def lines_inverse_kernel(me, windows, *refs):
    fields, refs = refs[:RADIX], refs[RADIX:]
    table, turn = refs[:2]
    later, (out, back, turned, final), held, done = refs[2:7], refs[7:11], refs[11:16], refs[16]
    cos_u, sin_u, pairs, cos_r, sin_r = held
    copies = fetch(later, held, done)
    rows, base = fields[0].shape[0] // 2, fields[0].shape[1]
    blocks, reach = pairs.shape[0], pairs.shape[1] // 2
    tail = pl.ds(RADIX * base, turned.shape[1] - RADIX * base)
    turned[:, tail, :] = jnp.zeros((2, tail.size, rows), bf16)
    for d, field in enumerate(fields):
        first = lax.dot_general(
            table[:, :base], field[:rows], (((1,), (1,)), ((), ())), preferred_element_type=f32
        )
        second = lax.dot_general(
            table[:, base:], field[rows:], (((1,), (1,)), ((), ())), preferred_element_type=f32
        )
        back[(me[0] + RADIX - d) % RADIX] = first + second
    for copy in copies:
        copy.wait()

    def aft(tile, carry):
        at = pl.multiple_of(tile * 16, 16)
        for lane in range(0, rows, 128):
            here = pl.ds(lane, 128)
            parts = []
            for k in range(RADIX):
                cosine = turn[pl.ds(at, 16), 2 * k : 2 * k + 1]
                sine = turn[pl.ds(at, 16), 2 * k + 1 : 2 * k + 2]
                value = (back[k, pl.ds(at, 16), here], back[k, pl.ds(base + at, 16), here])
                parts.append(twist(value, cosine, sine, 1))
            for a, (real, imag) in enumerate(fft8(parts, 1)):
                cell = pl.ds(a * base + at, 16)
                cosine, sine = cos_u[cell, here], sin_u[cell, here]
                u_re = (real * cosine - imag * sine).astype(bf16)
                u_im = (real * sine + imag * cosine).astype(bf16)
                turned[0, cell, here] = u_re
                turned[1, cell, here] = u_im
                final[0, cell, here] = u_re.astype(f32)
                final[1, cell, here] = u_im.astype(f32)
        return carry

    lax.fori_loop(0, base // 16, aft, 0)

    def some_blocks(group, carry):
        cells, changes = [], []
        for one in range(BLOCK_GROUP):
            c = group * BLOCK_GROUP + one
            cell = pl.ds(pl.multiple_of(windows[c] * 16, 16), reach)
            both = jnp.concatenate([turned[0, cell, :], turned[1, cell, :]], axis=0)
            cells.append(cell)
            changes.append(jnp.dot(pairs[c], both, preferred_element_type=f32))
        for cell, change in zip(cells, changes):
            final[0, cell, :] += change[:reach]
            final[1, cell, :] += change[reach:]
        return carry

    lax.fori_loop(0, blocks // BLOCK_GROUP, some_blocks, 0)

    def image(tile, carry):
        cell = pl.ds(pl.multiple_of(tile * 16, 16), 16)
        across, _, along, piece = out.shape[:4]
        owner, place = tile * 16 // piece, tile * 16 % piece
        spot = pl.ds(pl.multiple_of(place, 16), 16)
        out[owner // along % across, owner // (along * across), owner % along, spot, :] = (
            final[0, cell, :] * cos_r[cell, :] - final[1, cell, :] * sin_r[cell, :]
        ).astype(bf16)
        return carry

    lax.fori_loop(0, RADIX * base // 16, image, 0)


def call(kernel, out_shape, scratch, *operands, scalars=0, later=0):
    anywhere = pl.BlockSpec(memory_space=pl.ANY)
    smem = pl.BlockSpec(memory_space=pltpu.SMEM)
    vmem = pl.BlockSpec(memory_space=pltpu.VMEM)
    return pl.pallas_call(
        kernel,
        out_shape=out_shape,
        in_specs=[smem] * scalars
        + [vmem] * (len(operands) - scalars - later)
        + [anywhere] * later,
        out_specs=jax.tree.map(lambda _: vmem, out_shape),
        scratch_shapes=scratch,
        interpret=INTERPRET,
    )(*operands)


def cos_sin(angle):
    quarters = jnp.round(angle * (2.0 / math.pi))
    rest = angle - quarters * 1.5703125
    rest = rest - quarters * 4.837512969970703125e-4
    rest = rest - quarters * 7.549789948768648e-8
    square = rest * rest
    sine = ((-1.9515295891e-4 * square + 8.3321608736e-3) * square - 1.6666654611e-1) * square
    sine = sine * rest + rest
    cosine = (2.443315711809948e-5 * square - 1.388731625493765e-3) * square
    cosine = (cosine + 4.166664568298827e-2) * (square * square) - 0.5 * square + 1.0
    count = quarters.astype(jnp.int32)
    odd = (count & 1) != 0
    first = jnp.where(odd, sine, cosine)
    second = jnp.where(odd, cosine, sine)
    return (
        jnp.where(((count + 1) & 2) != 0, -first, first),
        jnp.where((count & 2) != 0, -second, second),
    )


def wave_numbers(indices, extent):
    signed = jnp.where(indices < extent // 2, indices, indices - extent)
    return signed.astype(f32) * (2.0 * math.pi / (extent * grid_step))


def propagator(angular, cut_index, extent_x, extent_y):
    cross_ids = (
        jnp.arange(RADIX, dtype=jnp.int32)[:, None]
        + RADIX * jnp.arange(extent_x // RADIX, dtype=jnp.int32)[None, :]
    )
    line_ids = cut_index + RADIX * jnp.arange(extent_y // RADIX, dtype=jnp.int32)
    wave_x = wave_numbers(cross_ids, extent_x)
    wave_y = wave_numbers(line_ids, extent_y)
    vertical = (angular * slow_ref) ** 2 - wave_x[:, :, None] ** 2 - wave_y[None, None, :] ** 2
    root_abs = jnp.sqrt(jnp.abs(vertical))
    cosine, sine = cos_sin(root_abs * depth_step)
    real_part = jnp.where(vertical > 0, cosine, jnp.exp(-root_abs * depth_step))
    imag_part = jnp.where(vertical > 0, sine, jnp.zeros_like(root_abs))
    return (real_part, imag_part)


def rotate(values, axes):
    size = math.prod(lax.axis_size(axis) for axis in axes)
    got = [values[0]]
    for d in range(1, size):
        got.append(lax.ppermute(values[d], axes, [(i, (i + d) % size) for i in range(size)]))
    return got


def split(value, axis, owner):
    size = lax.axis_size(axis)
    shaped = value.reshape((size, value.shape[0] // size) + value.shape[1:])
    shaped = lax.all_to_all(shaped, axis, 0, 0)
    return lax.dynamic_index_in_dim(shaped, owner, 0, keepdims=False)


def join(piece, axis):
    copies = jnp.broadcast_to(piece[None], (lax.axis_size(axis),) + piece.shape)
    copies = lax.all_to_all(copies, axis, 0, 0)
    return copies.reshape((-1,) + piece.shape[1:])


def swap(value, axis, bit):
    return lax.ppermute(value, axis, [(i, i ^ bit) for i in range(lax.axis_size(axis))])


def from_owner(value, owner_id):
    across, along = lax.axis_size("x"), lax.axis_size("z")
    piece = split(value, "x", owner_id // along % across)
    piece = split(piece, "z", owner_id % along)
    if lax.axis_size("yh") > 1:
        other = swap(piece, "yh", 1)
        same = lax.axis_index("yh") == owner_id // (across * along)
        piece = jnp.where(same, piece, other)
    return piece


def sum_over(part, axis, kind):
    terms = lax.all_to_all(part, axis, 0, 0, tiled=True)
    return jnp.sum(terms.astype(f32), axis=0).astype(kind)


def block_windows(matrices, starts, lengths):
    capacity = matrices.shape[2]
    reach = capacity + 16
    windows = starts // 16
    slots = jnp.arange(capacity, dtype=jnp.int32)
    spots = jnp.arange(reach, dtype=jnp.int32)
    place = (spots[None, :, None] == slots[None, None, :] + (starts % 16)[:, None, None]) & (
        slots[None, None, :] < lengths[:, None, None]
    )
    place = place.astype(bf16)
    moved = jnp.einsum("cia,dcab->dcib", place, matrices, preferred_element_type=f32).astype(bf16)
    moved = jnp.einsum("dcib,cjb->dcij", moved, place, preferred_element_type=f32).astype(bf16)
    upper = jnp.concatenate([moved[0], -moved[1]], axis=2)
    lower = jnp.concatenate([moved[1], moved[0]], axis=2)
    return windows, jnp.concatenate([upper, lower], axis=1)


def step(wavefield, slowness, block_inverse, block_lengths, slab_owner, shot_position):
    counts = tuple(lax.axis_size(name) for name in FREQ_AXES)
    freq_total = math.prod(counts)
    cut_count = lax.axis_size("yl") * lax.axis_size("core")
    row_count, extent_y = wavefield.shape[2], wavefield.shape[3]
    extent_x = row_count * cut_count
    base = extent_y // RADIX
    freq_index = lax.axis_index(FREQ_AXES)
    cut_index = lax.axis_index(CUT_AXES)
    device = cut_index.reshape(1).astype(jnp.int32)
    angular = (
        2.0 * math.pi * (band_low + band_width * (freq_index.astype(f32) + 0.5) / freq_total)
    )
    inverse, turn = dft_tables(extent_y)
    turn_rows = turn[:, :base]
    turn_here = lax.dynamic_slice_in_dim(turn, cut_index * base, base, 1).T
    turn_cols = turn_rows.T
    chunk = jax.ShapeDtypeStruct((2 * row_count, base), bf16)

    spectrum = call(
        lines_forward_kernel,
        [chunk] * RADIX,
        [pltpu.VMEM((RADIX, row_count, 2 * base), bf16)],
        device, wavefield[0], inverse, turn_rows,
        scalars=1,
    )
    columns = rotate(spectrum, CUT_AXES)

    prop_re, prop_im = propagator(angular, cut_index, extent_x, extent_y)
    rows_x = cut_index * row_count + jnp.arange(row_count, dtype=jnp.int32)
    offset_x = (rows_x - shot_position[0]).astype(f32) * grid_step
    offset_y = (jnp.arange(extent_y, dtype=jnp.int32) - shot_position[1]).astype(f32) * grid_step
    distance = jnp.sqrt(
        offset_x[None, :] ** 2 + offset_y[:, None] ** 2 + depth_step * depth_step
    )
    ray = angular * slow_ref * distance
    level = 1.0 / math.sqrt(freq_total)
    cos_r, sin_r = cos_sin(ray)
    cos_r, sin_r = cos_r * level, sin_r * level
    owner_id = slab_owner[0]
    pieces = counts[1] * counts[2] * 16
    joined = jnp.concatenate([slowness[0].T, block_inverse[0].reshape(-1, row_count)], axis=0)
    filled = joined.shape[0]
    joined = jnp.pad(joined, ((0, -filled % pieces), (0, 0)))
    share = join(from_owner(joined, owner_id), "z")
    columns, prop_re, prop_im, cos_r, sin_r, share = lax.optimization_barrier(
        (columns, prop_re, prop_im, cos_r, sin_r, share)
    )

    restored = call(
        across_kernel,
        [chunk] * RADIX,
        [
            pltpu.VMEM((RADIX, 2 * row_count, base), bf16),
            pltpu.VMEM((RADIX, 2 * row_count, base), f32),
            pltpu.VMEM(prop_re.shape, f32),
            pltpu.VMEM(prop_im.shape, f32),
            pltpu.SemaphoreType.DMA((2,)),
        ],
        *columns, inverse, turn_here, prop_re, prop_im,
        later=2,
    )
    row_field = rotate(restored, CUT_AXES)

    joined, _ = lax.optimization_barrier((join(share, "x"), restored[0]))
    mine = joined[extent_y:filled]
    other = swap(mine, "core", 1)
    first = lax.axis_index("core") == 0
    operators = jnp.concatenate(
        [jnp.where(first, mine, other), jnp.where(first, other, mine)], axis=0
    )
    operators = join(operators, "yl")
    shape = block_inverse.shape
    matrices = operators.reshape((cut_count,) + shape[1:]).transpose(1, 0, 2, 3, 4)
    matrices = matrices.reshape(2, -1, shape[3], shape[4])
    lengths = lax.dynamic_index_in_dim(block_lengths, owner_id, 0, keepdims=False)
    starts = jnp.cumsum(lengths) - lengths
    windows, pairs = block_windows(matrices, starts, lengths)
    phases = angular * depth_step * (joined[:extent_y].astype(f32) - slow_ref)
    cos_u, sin_u = cos_sin(phases)

    late = (cos_u, sin_u, pairs, cos_r, sin_r)
    part = call(
        lines_inverse_kernel,
        jax.ShapeDtypeStruct(
            (counts[1], counts[0], counts[2], extent_y // freq_total, row_count), bf16
        ),
        [
            pltpu.VMEM((RADIX, 2 * base, row_count), f32),
            pltpu.VMEM((2, extent_y + shape[3], row_count), bf16),
            pltpu.VMEM((2, extent_y + shape[3], row_count), f32),
            *[pltpu.VMEM(value.shape, value.dtype) for value in late],
            pltpu.SemaphoreType.DMA((len(late),)),
        ],
        device, windows, *row_field, inverse, turn_cols, *late,
        scalars=2,
        later=len(late),
    )
    part = sum_over(part, "x", bf16)
    part = part.reshape((counts[0] * counts[2],) + part.shape[2:])
    image = sum_over(part, ("yh", "z"), f32)
    return image.T[None]


def solution(mesh):
    sizes = {"yh": 2, "x": 4, "z": 8, "yl": 4, "core": 2}
    if mesh.devices.size != math.prod(sizes.values()):
        sizes = {"yh": 1, "x": 1, "z": 1, "yl": 4, "core": 2}
    fine = Mesh(mesh.devices.reshape(tuple(sizes.values())), tuple(sizes))
    placed = (
        P(FREQ_AXES, None, CUT_AXES, None),
        P(FREQ_AXES, CUT_AXES, None),
        P(FREQ_AXES, None, CUT_AXES, None, None),
        P(),
        P(),
        P(),
    )
    return jax.shard_map(
        step, mesh=fine, in_specs=placed, out_specs=P(None, CUT_AXES, FREQ_AXES), check_vma=False
    )
```

```python
import math

import jax
import jax.numpy as jnp
import numpy as np
from jax import lax
from jax.experimental import pallas as pl
from jax.experimental.pallas import tpu as pltpu
from jax.sharding import Mesh, PartitionSpec as P

grid_step = 0.0125
depth_step = 0.02
slow_ref = 0.4
band_low = 5.0
band_width = 55.0

INTERPRET = False
FREQ_AXES = ("yh", "x", "z")
CUT_AXES = ("yl", "core")
RADIX = 8
f32 = jnp.float32
bf16 = jnp.bfloat16


def dft_tables(extent):
    base = extent // RADIX
    ids = np.arange(base)
    angle = 2.0 * np.pi / base * ((ids[:, None] * ids[None, :]) % base)
    cosine = np.cos(angle) / math.sqrt(base)
    sine = np.sin(angle) / math.sqrt(base)
    inverse = np.block([[cosine, -sine], [sine, cosine]])
    twists = 2.0 * np.pi / extent * (np.arange(RADIX)[:, None] * np.arange(extent)[None, :])
    turn = np.stack([np.cos(twists), np.sin(twists)], axis=1) / math.sqrt(RADIX)
    turn = turn.reshape(2 * RADIX, extent).astype(np.float32)
    return jnp.asarray(inverse, bf16), jnp.asarray(turn)


def fft4(parts, s):
    (r0, i0), (r1, i1), (r2, i2), (r3, i3) = parts
    ar, ai, br, bi = r0 + r2, i0 + i2, r0 - r2, i0 - i2
    cr, ci, dr, di = r1 + r3, i1 + i3, r1 - r3, i1 - i3
    if s > 0:
        one, three = (br - di, bi + dr), (br + di, bi - dr)
    else:
        one, three = (br + di, bi - dr), (br - di, bi + dr)
    return [(ar + cr, ai + ci), one, (ar - cr, ai - ci), three]


def fft8(parts, s):
    even = fft4(parts[0::2], s)
    odd = fft4(parts[1::2], s)
    half = math.sqrt(0.5)
    (r0, i0), (r1, i1), (r2, i2), (r3, i3) = odd
    if s > 0:
        turned = [
            (r0, i0),
            ((r1 - i1) * half, (i1 + r1) * half),
            (-i2, r2),
            ((r3 + i3) * -half, (r3 - i3) * half),
        ]
    else:
        turned = [
            (r0, i0),
            ((r1 + i1) * half, (i1 - r1) * half),
            (i2, -r2),
            ((i3 - r3) * half, (r3 + i3) * -half),
        ]
    low = [(e[0] + t[0], e[1] + t[1]) for e, t in zip(even, turned)]
    high = [(e[0] - t[0], e[1] - t[1]) for e, t in zip(even, turned)]
    return low + high


def twist(value, cosine, sine, s):
    real, imag = value
    if s > 0:
        return (real * cosine - imag * sine, imag * cosine + real * sine)
    return (real * cosine + imag * sine, imag * cosine - real * sine)


def fetch(sources, targets, done):
    copies = [
        pltpu.make_async_copy(source, target, done.at[i])
        for i, (source, target) in enumerate(zip(sources, targets))
    ]
    for copy in copies:
        copy.start()
    return copies


def lines_forward_kernel(me, field, table, turn, *outs_mid):
    outs, mid = outs_mid[:RADIX], outs_mid[RADIX]
    rows, base = mid.shape[1], mid.shape[2] // 2

    def step(tile, carry):
        at = pl.ds(pl.multiple_of(tile * 16, 16), 16)
        for lane in range(0, base, 128):
            parts = []
            for a in range(RADIX):
                here = pl.ds(a * base + lane, 128)
                parts.append((field[0, at, here].astype(f32), field[1, at, here].astype(f32)))
            for k, value in enumerate(fft8(parts, -1)):
                cosine = turn[2 * k : 2 * k + 1, lane : lane + 128]
                sine = turn[2 * k + 1 : 2 * k + 2, lane : lane + 128]
                real, imag = twist(value, cosine, sine, -1)
                mid[k, at, pl.ds(lane, 128)] = real.astype(bf16)
                mid[k, at, pl.ds(base + lane, 128)] = imag.astype(bf16)
        return carry

    lax.fori_loop(0, rows // 16, step, 0)
    for d, out in enumerate(outs):
        both = jnp.dot(mid[(me[0] + d) % RADIX], table[...], preferred_element_type=f32)
        out[:rows] = both[:, :base].astype(bf16)
        out[rows:] = both[:, base:].astype(bf16)


def across_kernel(*refs):
    fields, refs = refs[:RADIX], refs[RADIX:]
    table, turn = refs[:2]
    later, refs = refs[2:4], refs[4:]
    outs, (mid, back, prop_re, prop_im, done) = refs[:RADIX], refs[RADIX:]
    copies = fetch(later, (prop_re, prop_im), done)
    base, cols = prop_re.shape[1], prop_re.shape[2]

    def fore(tile, carry):
        at = pl.multiple_of(tile * 16, 16)
        for lane in range(0, cols, 128):
            here = pl.ds(lane, 128)
            parts = []
            for field in fields:
                parts.append(
                    (
                        field[pl.ds(at, 16), here].astype(f32),
                        field[pl.ds(base + at, 16), here].astype(f32),
                    )
                )
            for k, value in enumerate(fft8(parts, 1)):
                cosine = turn[pl.ds(at, 16), 2 * k : 2 * k + 1]
                sine = turn[pl.ds(at, 16), 2 * k + 1 : 2 * k + 2]
                real, imag = twist(value, cosine, sine, -1)
                mid[k, pl.ds(at, 16), here] = real.astype(bf16)
                mid[k, pl.ds(base + at, 16), here] = (-imag).astype(bf16)
        return carry

    lax.fori_loop(0, base // 16, fore, 0)
    for copy in copies:
        copy.wait()

    def waves(step, carry):
        for k in (2 * step, 2 * step + 1):
            both = jnp.dot(table[...], mid[k], preferred_element_type=f32)
            real, minus = both[:base], both[base:]
            p_re, p_im = prop_re[k], prop_im[k]
            mid[k, :base] = (real * p_re + minus * p_im).astype(bf16)
            mid[k, base:] = (real * p_im - minus * p_re).astype(bf16)
            back[k] = jnp.dot(table[...], mid[k], preferred_element_type=f32)
        return carry

    lax.fori_loop(0, RADIX // 2, waves, 0)

    def aft(tile, carry):
        at = pl.multiple_of(tile * 16, 16)
        for lane in range(0, cols, 128):
            here = pl.ds(lane, 128)
            parts = []
            for k in range(RADIX):
                cosine = turn[pl.ds(at, 16), 2 * k : 2 * k + 1]
                sine = turn[pl.ds(at, 16), 2 * k + 1 : 2 * k + 2]
                value = (back[k, pl.ds(at, 16), here], back[k, pl.ds(base + at, 16), here])
                parts.append(twist(value, cosine, sine, 1))
            for out, (real, imag) in zip(outs, fft8(parts, 1)):
                out[pl.ds(at, 16), here] = real.astype(bf16)
                out[pl.ds(base + at, 16), here] = imag.astype(bf16)
        return carry

    lax.fori_loop(0, base // 16, aft, 0)


def lines_inverse_kernel(me, starts, lengths, *refs):
    fields, refs = refs[:RADIX], refs[RADIX:]
    table, turn = refs[:2]
    later, (out, back, turned, final), held, done = refs[2:7], refs[7:11], refs[11:16], refs[16]
    cos_u, sin_u, matrices, cos_r, sin_r = held
    copies = fetch(later, held, done)
    rows, base = fields[0].shape[0] // 2, fields[0].shape[1]
    cuts, _, share, capacity = matrices.shape[:4]
    reach = capacity + 16
    tail = pl.ds(RADIX * base, turned.shape[1] - RADIX * base)
    turned[:, tail, :] = jnp.zeros((2, tail.size, rows), bf16)
    final[:, tail, :] = jnp.zeros((2, tail.size, rows), f32)
    for d, field in enumerate(fields):
        first = lax.dot_general(
            table[:, :base], field[:rows], (((1,), (1,)), ((), ())), preferred_element_type=f32
        )
        second = lax.dot_general(
            table[:, base:], field[rows:], (((1,), (1,)), ((), ())), preferred_element_type=f32
        )
        back[(me[0] + RADIX - d) % RADIX] = first + second
    for copy in copies:
        copy.wait()

    def aft(tile, carry):
        at = pl.multiple_of(tile * 16, 16)
        for lane in range(0, rows, 128):
            here = pl.ds(lane, 128)
            parts = []
            for k in range(RADIX):
                cosine = turn[pl.ds(at, 16), 2 * k : 2 * k + 1]
                sine = turn[pl.ds(at, 16), 2 * k + 1 : 2 * k + 2]
                value = (back[k, pl.ds(at, 16), here], back[k, pl.ds(base + at, 16), here])
                parts.append(twist(value, cosine, sine, 1))
            for a, (real, imag) in enumerate(fft8(parts, 1)):
                cell = pl.ds(a * base + at, 16)
                cosine, sine = cos_u[cell, here], sin_u[cell, here]
                u_re = (real * cosine - imag * sine).astype(bf16)
                u_im = (real * sine + imag * cosine).astype(bf16)
                turned[0, cell, here] = u_re
                turned[1, cell, here] = u_im
                final[0, cell, here] = u_re.astype(f32)
                final[1, cell, here] = u_im.astype(f32)
        return carry

    lax.fori_loop(0, base // 16, aft, 0)

    spot = lax.broadcasted_iota(jnp.int32, (reach, rows), 0)

    def some_blocks(cut, carry):
        cells, changes = [], []
        for one in range(share):
            c = cut * share + one
            start, length = starts[c], lengths[c]
            cell = pl.ds(pl.multiple_of(start // 16 * 16, 16), reach)
            offset = start % 16
            lift = jnp.where(offset == 0, 0, reach - offset)
            inside = spot < length
            parts = []
            for part in range(2):
                window = pltpu.roll(turned[part, cell, :].astype(f32), lift, 0)
                parts.append(jnp.where(inside, window, 0.0)[:capacity].astype(bf16))
            both = jnp.concatenate([matrices[cut, 0, one], matrices[cut, 1, one]], axis=0)
            by_re = jnp.dot(both, parts[0], preferred_element_type=f32)
            by_im = jnp.dot(both, parts[1], preferred_element_type=f32)
            change = (
                by_re[:capacity] - by_im[capacity:],
                by_re[capacity:] + by_im[:capacity],
            )
            moved = []
            for value in change:
                value = jnp.concatenate([value, jnp.zeros((16, rows), f32)], axis=0)
                moved.append(pltpu.roll(jnp.where(inside, value, 0.0), offset, 0))
            cells.append(cell)
            changes.append(moved)
        for cell, change in zip(cells, changes):
            final[0, cell, :] += change[0]
            final[1, cell, :] += change[1]
        return carry

    lax.fori_loop(0, cuts, some_blocks, 0)

    def image(tile, carry):
        cell = pl.ds(pl.multiple_of(tile * 16, 16), 16)
        across, _, along, piece = out.shape[:4]
        owner, place = tile * 16 // piece, tile * 16 % piece
        spot = pl.ds(pl.multiple_of(place, 16), 16)
        out[owner // along % across, owner // (along * across), owner % along, spot, :] = (
            final[0, cell, :] * cos_r[cell, :] - final[1, cell, :] * sin_r[cell, :]
        ).astype(bf16)
        return carry

    lax.fori_loop(0, RADIX * base // 16, image, 0, unroll=4)


def call(kernel, out_shape, scratch, *operands, scalars=0, later=0):
    anywhere = pl.BlockSpec(memory_space=pl.ANY)
    smem = pl.BlockSpec(memory_space=pltpu.SMEM)
    vmem = pl.BlockSpec(memory_space=pltpu.VMEM)
    return pl.pallas_call(
        kernel,
        out_shape=out_shape,
        in_specs=[smem] * scalars
        + [vmem] * (len(operands) - scalars - later)
        + [anywhere] * later,
        out_specs=jax.tree.map(lambda _: vmem, out_shape),
        scratch_shapes=scratch,
        interpret=INTERPRET,
    )(*operands)


def cos_sin(angle):
    quarters = jnp.round(angle * (2.0 / math.pi))
    rest = angle - quarters * 1.5703125
    rest = rest - quarters * 4.837512969970703125e-4
    rest = rest - quarters * 7.549789948768648e-8
    square = rest * rest
    sine = ((-1.9515295891e-4 * square + 8.3321608736e-3) * square - 1.6666654611e-1) * square
    sine = sine * rest + rest
    cosine = (2.443315711809948e-5 * square - 1.388731625493765e-3) * square
    cosine = (cosine + 4.166664568298827e-2) * (square * square) - 0.5 * square + 1.0
    count = quarters.astype(jnp.int32)
    odd = (count & 1) != 0
    first = jnp.where(odd, sine, cosine)
    second = jnp.where(odd, cosine, sine)
    return (
        jnp.where(((count + 1) & 2) != 0, -first, first),
        jnp.where((count & 2) != 0, -second, second),
    )


def wave_numbers(indices, extent):
    signed = jnp.where(indices < extent // 2, indices, indices - extent)
    return signed.astype(f32) * (2.0 * math.pi / (extent * grid_step))


def propagator(angular, cut_index, extent_x, extent_y):
    cross_ids = (
        jnp.arange(RADIX, dtype=jnp.int32)[:, None]
        + RADIX * jnp.arange(extent_x // RADIX, dtype=jnp.int32)[None, :]
    )
    line_ids = cut_index + RADIX * jnp.arange(extent_y // RADIX, dtype=jnp.int32)
    wave_x = wave_numbers(cross_ids, extent_x)
    wave_y = wave_numbers(line_ids, extent_y)
    vertical = (angular * slow_ref) ** 2 - wave_x[:, :, None] ** 2 - wave_y[None, None, :] ** 2
    root_abs = jnp.sqrt(jnp.abs(vertical))
    cosine, sine = cos_sin(root_abs * depth_step)
    real_part = jnp.where(vertical > 0, cosine, jnp.exp(-root_abs * depth_step))
    imag_part = jnp.where(vertical > 0, sine, jnp.zeros_like(root_abs))
    return (real_part, imag_part)


def rotate(values, axes):
    size = math.prod(lax.axis_size(axis) for axis in axes)
    got = [values[0]]
    for d in range(1, size):
        got.append(lax.ppermute(values[d], axes, [(i, (i + d) % size) for i in range(size)]))
    return got


def split(value, axis, owner):
    size = lax.axis_size(axis)
    shaped = value.reshape((size, value.shape[0] // size) + value.shape[1:])
    shaped = lax.all_to_all(shaped, axis, 0, 0)
    return lax.dynamic_index_in_dim(shaped, owner, 0, keepdims=False)


def join(piece, axis):
    copies = jnp.broadcast_to(piece[None], (lax.axis_size(axis),) + piece.shape)
    copies = lax.all_to_all(copies, axis, 0, 0)
    return copies.reshape((-1,) + piece.shape[1:])


def swap(value, axis, bit):
    return lax.ppermute(value, axis, [(i, i ^ bit) for i in range(lax.axis_size(axis))])


def from_owner(value, owner_id):
    across, along = lax.axis_size("x"), lax.axis_size("z")
    piece = split(value, "x", owner_id // along % across)
    piece = split(piece, "z", owner_id % along)
    if lax.axis_size("yh") > 1:
        other = swap(piece, "yh", 1)
        same = lax.axis_index("yh") == owner_id // (across * along)
        piece = jnp.where(same, piece, other)
    return piece


def sum_over(part, axis, kind):
    terms = lax.all_to_all(part, axis, 0, 0, tiled=True)
    return jnp.sum(terms.astype(f32), axis=0).astype(kind)


def step(wavefield, slowness, block_inverse, block_lengths, slab_owner, shot_position):
    counts = tuple(lax.axis_size(name) for name in FREQ_AXES)
    freq_total = math.prod(counts)
    cut_count = lax.axis_size("yl") * lax.axis_size("core")
    row_count, extent_y = wavefield.shape[2], wavefield.shape[3]
    extent_x = row_count * cut_count
    base = extent_y // RADIX
    freq_index = lax.axis_index(FREQ_AXES)
    cut_index = lax.axis_index(CUT_AXES)
    device = cut_index.reshape(1).astype(jnp.int32)
    angular = (
        2.0 * math.pi * (band_low + band_width * (freq_index.astype(f32) + 0.5) / freq_total)
    )
    inverse, turn = dft_tables(extent_y)
    turn_rows = turn[:, :base]
    turn_here = lax.dynamic_slice_in_dim(turn, cut_index * base, base, 1).T
    turn_cols = turn_rows.T
    chunk = jax.ShapeDtypeStruct((2 * row_count, base), bf16)

    spectrum = call(
        lines_forward_kernel,
        [chunk] * RADIX,
        [pltpu.VMEM((RADIX, row_count, 2 * base), bf16)],
        device, wavefield[0], inverse, turn_rows,
        scalars=1,
    )
    columns = rotate(spectrum, CUT_AXES)

    prop_re, prop_im = propagator(angular, cut_index, extent_x, extent_y)
    rows_x = cut_index * row_count + jnp.arange(row_count, dtype=jnp.int32)
    offset_x = (rows_x - shot_position[0]).astype(f32) * grid_step
    offset_y = (jnp.arange(extent_y, dtype=jnp.int32) - shot_position[1]).astype(f32) * grid_step
    distance = jnp.sqrt(
        offset_x[None, :] ** 2 + offset_y[:, None] ** 2 + depth_step * depth_step
    )
    ray = angular * slow_ref * distance
    level = 1.0 / math.sqrt(freq_total)
    cos_r, sin_r = cos_sin(ray)
    cos_r, sin_r = cos_r * level, sin_r * level
    owner_id = slab_owner[0]
    pieces = counts[1] * counts[2] * 16
    joined = jnp.concatenate([slowness[0].T, block_inverse[0].reshape(-1, row_count)], axis=0)
    filled = joined.shape[0]
    joined = jnp.pad(joined, ((0, -filled % pieces), (0, 0)))
    share = join(from_owner(joined, owner_id), "z")
    restored = call(
        across_kernel,
        [chunk] * RADIX,
        [
            pltpu.VMEM((RADIX, 2 * row_count, base), bf16),
            pltpu.VMEM((RADIX, 2 * row_count, base), f32),
            pltpu.VMEM(prop_re.shape, f32),
            pltpu.VMEM(prop_im.shape, f32),
            pltpu.SemaphoreType.DMA((2,)),
        ],
        *columns, inverse, turn_here, prop_re, prop_im,
        later=2,
    )
    row_field = rotate(restored, CUT_AXES)

    share, _ = lax.optimization_barrier((share, restored[0]))
    joined = join(share, "x")
    mine = joined[extent_y:filled]
    other = swap(mine, "core", 1)
    first = lax.axis_index("core") == 0
    operators = jnp.concatenate(
        [jnp.where(first, mine, other), jnp.where(first, other, mine)], axis=0
    )
    operators = join(operators, "yl")
    shape = block_inverse.shape
    matrices = operators.reshape((cut_count,) + shape[1:])
    lengths = lax.dynamic_index_in_dim(block_lengths, owner_id, 0, keepdims=False)
    starts = jnp.cumsum(lengths) - lengths
    phases = angular * depth_step * (joined[:extent_y].astype(f32) - slow_ref)
    cos_u, sin_u = cos_sin(phases)

    late = (cos_u, sin_u, matrices, cos_r, sin_r)
    part = call(
        lines_inverse_kernel,
        jax.ShapeDtypeStruct(
            (counts[1], counts[0], counts[2], extent_y // freq_total, row_count), bf16
        ),
        [
            pltpu.VMEM((RADIX, 2 * base, row_count), f32),
            pltpu.VMEM((2, extent_y + shape[3], row_count), bf16),
            pltpu.VMEM((2, extent_y + shape[3], row_count), f32),
            *[pltpu.VMEM(value.shape, value.dtype) for value in late],
            pltpu.SemaphoreType.DMA((len(late),)),
        ],
        device, starts, lengths, *row_field, inverse, turn_cols, *late,
        scalars=3,
        later=len(late),
    )
    part = sum_over(part, "x", bf16)
    part = part.reshape((counts[0] * counts[2],) + part.shape[2:])
    image = sum_over(part, ("yh", "z"), f32)
    return image.T[None]


def solution(mesh):
    sizes = {"yh": 2, "x": 4, "z": 8, "yl": 4, "core": 2}
    if mesh.devices.size != math.prod(sizes.values()):
        sizes = {"yh": 1, "x": 1, "z": 1, "yl": 4, "core": 2}
    fine = Mesh(mesh.devices.reshape(tuple(sizes.values())), tuple(sizes))
    placed = (
        P(FREQ_AXES, None, CUT_AXES, None),
        P(FREQ_AXES, CUT_AXES, None),
        P(FREQ_AXES, None, CUT_AXES, None, None),
        P(),
        P(),
        P(),
    )
    return jax.shard_map(
        step, mesh=fine, in_specs=placed, out_specs=P(None, CUT_AXES, FREQ_AXES), check_vma=False
    )
```

```python
import math

import jax
import jax.numpy as jnp
import numpy as np
from jax import lax
from jax.experimental import pallas as pl
from jax.experimental.pallas import tpu as pltpu
from jax.sharding import Mesh, PartitionSpec as P

grid_step = 0.0125
depth_step = 0.02
slow_ref = 0.4
band_low = 5.0
band_width = 55.0

INTERPRET = False
FREQ_AXES = ("yh", "x", "z")
CUT_AXES = ("yl", "core")
RADIX = 8
f32 = jnp.float32
bf16 = jnp.bfloat16


def dft_tables(extent):
    base = extent // RADIX
    ids = np.arange(base)
    angle = 2.0 * np.pi / base * ((ids[:, None] * ids[None, :]) % base)
    cosine = np.cos(angle) / math.sqrt(base)
    sine = np.sin(angle) / math.sqrt(base)
    inverse = np.block([[cosine, -sine], [sine, cosine]])
    twists = 2.0 * np.pi / extent * (np.arange(RADIX)[:, None] * np.arange(extent)[None, :])
    turn = np.stack([np.cos(twists), np.sin(twists)], axis=1) / math.sqrt(RADIX)
    turn = turn.reshape(2 * RADIX, extent).astype(np.float32)
    return jnp.asarray(inverse, bf16), jnp.asarray(turn)


def fft4(parts, s):
    (r0, i0), (r1, i1), (r2, i2), (r3, i3) = parts
    ar, ai, br, bi = r0 + r2, i0 + i2, r0 - r2, i0 - i2
    cr, ci, dr, di = r1 + r3, i1 + i3, r1 - r3, i1 - i3
    if s > 0:
        one, three = (br - di, bi + dr), (br + di, bi - dr)
    else:
        one, three = (br + di, bi - dr), (br - di, bi + dr)
    return [(ar + cr, ai + ci), one, (ar - cr, ai - ci), three]


def fft8(parts, s):
    even = fft4(parts[0::2], s)
    odd = fft4(parts[1::2], s)
    half = math.sqrt(0.5)
    (r0, i0), (r1, i1), (r2, i2), (r3, i3) = odd
    if s > 0:
        turned = [
            (r0, i0),
            ((r1 - i1) * half, (i1 + r1) * half),
            (-i2, r2),
            ((r3 + i3) * -half, (r3 - i3) * half),
        ]
    else:
        turned = [
            (r0, i0),
            ((r1 + i1) * half, (i1 - r1) * half),
            (i2, -r2),
            ((i3 - r3) * half, (r3 + i3) * -half),
        ]
    low = [(e[0] + t[0], e[1] + t[1]) for e, t in zip(even, turned)]
    high = [(e[0] - t[0], e[1] - t[1]) for e, t in zip(even, turned)]
    return low + high


def twist(value, cosine, sine, s):
    real, imag = value
    if s > 0:
        return (real * cosine - imag * sine, imag * cosine + real * sine)
    return (real * cosine + imag * sine, imag * cosine - real * sine)


def fetch(sources, targets, done):
    copies = [
        pltpu.make_async_copy(source, target, done.at[i])
        for i, (source, target) in enumerate(zip(sources, targets))
    ]
    for copy in copies:
        copy.start()
    return copies


def lines_forward_kernel(me, field, table, turn, *outs_mid):
    outs, mid = outs_mid[:RADIX], outs_mid[RADIX]
    rows, base = mid.shape[1], mid.shape[2] // 2

    def step(tile, carry):
        at = pl.ds(pl.multiple_of(tile * 16, 16), 16)
        for lane in range(0, base, 128):
            parts = []
            for a in range(RADIX):
                here = pl.ds(a * base + lane, 128)
                parts.append((field[0, at, here].astype(f32), field[1, at, here].astype(f32)))
            for k, value in enumerate(fft8(parts, -1)):
                cosine = turn[2 * k : 2 * k + 1, lane : lane + 128]
                sine = turn[2 * k + 1 : 2 * k + 2, lane : lane + 128]
                real, imag = twist(value, cosine, sine, -1)
                mid[k, at, pl.ds(lane, 128)] = real.astype(bf16)
                mid[k, at, pl.ds(base + lane, 128)] = imag.astype(bf16)
        return carry

    lax.fori_loop(0, rows // 16, step, 0)
    for d, out in enumerate(outs):
        both = jnp.dot(mid[(me[0] + d) % RADIX], table[...], preferred_element_type=f32)
        out[:rows] = both[:, :base].astype(bf16)
        out[rows:] = both[:, base:].astype(bf16)


def across_kernel(*refs):
    fields, refs = refs[:RADIX], refs[RADIX:]
    table, turn = refs[:2]
    later, refs = refs[2:4], refs[4:]
    outs, (mid, back, prop_re, prop_im, done) = refs[:RADIX], refs[RADIX:]
    copies = fetch(later, (prop_re, prop_im), done)
    base, cols = prop_re.shape[1], prop_re.shape[2]

    def fore(tile, carry):
        at = pl.multiple_of(tile * 16, 16)
        for lane in range(0, cols, 128):
            here = pl.ds(lane, 128)
            parts = []
            for field in fields:
                parts.append(
                    (
                        field[pl.ds(at, 16), here].astype(f32),
                        field[pl.ds(base + at, 16), here].astype(f32),
                    )
                )
            for k, value in enumerate(fft8(parts, 1)):
                cosine = turn[pl.ds(at, 16), 2 * k : 2 * k + 1]
                sine = turn[pl.ds(at, 16), 2 * k + 1 : 2 * k + 2]
                real, imag = twist(value, cosine, sine, -1)
                mid[k, pl.ds(at, 16), here] = real.astype(bf16)
                mid[k, pl.ds(base + at, 16), here] = (-imag).astype(bf16)
        return carry

    lax.fori_loop(0, base // 16, fore, 0)
    for copy in copies:
        copy.wait()

    def waves(step, carry):
        for k in (2 * step, 2 * step + 1):
            both = jnp.dot(table[...], mid[k], preferred_element_type=f32)
            real, minus = both[:base], both[base:]
            p_re, p_im = prop_re[k], prop_im[k]
            mid[k, :base] = (real * p_re + minus * p_im).astype(bf16)
            mid[k, base:] = (real * p_im - minus * p_re).astype(bf16)
            back[k] = jnp.dot(table[...], mid[k], preferred_element_type=f32)
        return carry

    lax.fori_loop(0, RADIX // 2, waves, 0)

    def aft(tile, carry):
        at = pl.multiple_of(tile * 16, 16)
        for lane in range(0, cols, 128):
            here = pl.ds(lane, 128)
            parts = []
            for k in range(RADIX):
                cosine = turn[pl.ds(at, 16), 2 * k : 2 * k + 1]
                sine = turn[pl.ds(at, 16), 2 * k + 1 : 2 * k + 2]
                value = (back[k, pl.ds(at, 16), here], back[k, pl.ds(base + at, 16), here])
                parts.append(twist(value, cosine, sine, 1))
            for out, (real, imag) in zip(outs, fft8(parts, 1)):
                out[pl.ds(at, 16), here] = real.astype(bf16)
                out[pl.ds(base + at, 16), here] = imag.astype(bf16)
        return carry

    lax.fori_loop(0, base // 16, aft, 0)


def lines_inverse_kernel(me, starts, lengths, *refs):
    fields, refs = refs[:RADIX], refs[RADIX:]
    table, turn = refs[:2]
    later, (out, back, turned, final), held, done = refs[2:7], refs[7:11], refs[11:16], refs[16]
    cos_u, sin_u, matrices, cos_r, sin_r = held
    copies = fetch(later, held, done)
    rows, base = fields[0].shape[0] // 2, fields[0].shape[1]
    cuts, _, share, capacity = matrices.shape[:4]
    reach = capacity + 16
    tail = pl.ds(RADIX * base, turned.shape[1] - RADIX * base)
    turned[:, tail, :] = jnp.zeros((2, tail.size, rows), bf16)
    final[:, tail, :] = jnp.zeros((2, tail.size, rows), f32)
    for d, field in enumerate(fields):
        first = lax.dot_general(
            table[:, :base], field[:rows], (((1,), (1,)), ((), ())), preferred_element_type=f32
        )
        second = lax.dot_general(
            table[:, base:], field[rows:], (((1,), (1,)), ((), ())), preferred_element_type=f32
        )
        back[(me[0] + RADIX - d) % RADIX] = first + second
    for copy in copies:
        copy.wait()

    def aft(tile, carry):
        at = pl.multiple_of(tile * 16, 16)
        for lane in range(0, rows, 128):
            here = pl.ds(lane, 128)
            parts = []
            for k in range(RADIX):
                cosine = turn[pl.ds(at, 16), 2 * k : 2 * k + 1]
                sine = turn[pl.ds(at, 16), 2 * k + 1 : 2 * k + 2]
                value = (back[k, pl.ds(at, 16), here], back[k, pl.ds(base + at, 16), here])
                parts.append(twist(value, cosine, sine, 1))
            for a, (real, imag) in enumerate(fft8(parts, 1)):
                cell = pl.ds(a * base + at, 16)
                cosine, sine = cos_u[cell, here], sin_u[cell, here]
                u_re = (real * cosine - imag * sine).astype(bf16)
                u_im = (real * sine + imag * cosine).astype(bf16)
                turned[0, cell, here] = u_re
                turned[1, cell, here] = u_im
                final[0, cell, here] = u_re.astype(f32)
                final[1, cell, here] = u_im.astype(f32)
        return carry

    lax.fori_loop(0, base // 16, aft, 0)

    lanes = matrices.shape[4]
    spot = lax.broadcasted_iota(jnp.int32, (capacity, lanes), 0)
    mate = lax.broadcasted_iota(jnp.int32, (capacity, lanes), 1)

    def some_blocks(cut, carry):
        cells, changes = [], []
        for one in range(share):
            c = cut * share + one
            start, length = starts[c], lengths[c]
            cell = pl.ds(pl.multiple_of(start // 16 * 16, 16), reach)
            inside = jnp.maximum(spot, mate) < length
            parts = []
            for part in range(2):
                value = jnp.where(inside, matrices[cut, part, one].astype(f32), 0.0)
                value = jnp.concatenate([value, jnp.zeros((reach - capacity, lanes), f32)], axis=0)
                value = pltpu.roll(pltpu.roll(value, start % 16, 0), start % 16, 1)
                parts.append(value[:, :reach].astype(bf16))
            both = jnp.concatenate(parts, axis=0)
            by_re = jnp.dot(both, turned[0, cell, :], preferred_element_type=f32)
            by_im = jnp.dot(both, turned[1, cell, :], preferred_element_type=f32)
            cells.append(cell)
            changes.append((by_re[:reach] - by_im[reach:], by_re[reach:] + by_im[:reach]))
        for cell, change in zip(cells, changes):
            final[0, cell, :] += change[0]
            final[1, cell, :] += change[1]
        return carry

    lax.fori_loop(0, cuts, some_blocks, 0)

    def image(tile, carry):
        cell = pl.ds(pl.multiple_of(tile * 16, 16), 16)
        across, _, along, piece = out.shape[:4]
        owner, place = tile * 16 // piece, tile * 16 % piece
        spot = pl.ds(pl.multiple_of(place, 16), 16)
        out[owner // along % across, owner // (along * across), owner % along, spot, :] = (
            final[0, cell, :] * cos_r[cell, :] - final[1, cell, :] * sin_r[cell, :]
        ).astype(bf16)
        return carry

    lax.fori_loop(0, RADIX * base // 16, image, 0, unroll=4)


def call(kernel, out_shape, scratch, *operands, scalars=0, later=0):
    anywhere = pl.BlockSpec(memory_space=pl.ANY)
    smem = pl.BlockSpec(memory_space=pltpu.SMEM)
    vmem = pl.BlockSpec(memory_space=pltpu.VMEM)
    return pl.pallas_call(
        kernel,
        out_shape=out_shape,
        in_specs=[smem] * scalars
        + [vmem] * (len(operands) - scalars - later)
        + [anywhere] * later,
        out_specs=jax.tree.map(lambda _: vmem, out_shape),
        scratch_shapes=scratch,
        interpret=INTERPRET,
    )(*operands)


def cos_sin(angle):
    quarters = jnp.round(angle * (2.0 / math.pi))
    rest = angle - quarters * 1.5703125
    rest = rest - quarters * 4.837512969970703125e-4
    rest = rest - quarters * 7.549789948768648e-8
    square = rest * rest
    sine = ((-1.9515295891e-4 * square + 8.3321608736e-3) * square - 1.6666654611e-1) * square
    sine = sine * rest + rest
    cosine = (2.443315711809948e-5 * square - 1.388731625493765e-3) * square
    cosine = (cosine + 4.166664568298827e-2) * (square * square) - 0.5 * square + 1.0
    count = quarters.astype(jnp.int32)
    odd = (count & 1) != 0
    first = jnp.where(odd, sine, cosine)
    second = jnp.where(odd, cosine, sine)
    return (
        jnp.where(((count + 1) & 2) != 0, -first, first),
        jnp.where((count & 2) != 0, -second, second),
    )


def wave_numbers(indices, extent):
    signed = jnp.where(indices < extent // 2, indices, indices - extent)
    return signed.astype(f32) * (2.0 * math.pi / (extent * grid_step))


def propagator(angular, cut_index, extent_x, extent_y):
    cross_ids = (
        jnp.arange(RADIX, dtype=jnp.int32)[:, None]
        + RADIX * jnp.arange(extent_x // RADIX, dtype=jnp.int32)[None, :]
    )
    line_ids = cut_index + RADIX * jnp.arange(extent_y // RADIX, dtype=jnp.int32)
    wave_x = wave_numbers(cross_ids, extent_x)
    wave_y = wave_numbers(line_ids, extent_y)
    vertical = (angular * slow_ref) ** 2 - wave_x[:, :, None] ** 2 - wave_y[None, None, :] ** 2
    root_abs = jnp.sqrt(jnp.abs(vertical))
    cosine, sine = cos_sin(root_abs * depth_step)
    real_part = jnp.where(vertical > 0, cosine, jnp.exp(-root_abs * depth_step))
    imag_part = jnp.where(vertical > 0, sine, jnp.zeros_like(root_abs))
    return (real_part, imag_part)


def rotate(values, axes):
    size = math.prod(lax.axis_size(axis) for axis in axes)
    got = [values[0]]
    for d in range(1, size):
        got.append(lax.ppermute(values[d], axes, [(i, (i + d) % size) for i in range(size)]))
    return got


def split(value, axis, owner):
    size = lax.axis_size(axis)
    shaped = value.reshape((size, value.shape[0] // size) + value.shape[1:])
    shaped = lax.all_to_all(shaped, axis, 0, 0)
    return lax.dynamic_index_in_dim(shaped, owner, 0, keepdims=False)


def join(piece, axis):
    copies = jnp.broadcast_to(piece[None], (lax.axis_size(axis),) + piece.shape)
    copies = lax.all_to_all(copies, axis, 0, 0)
    return copies.reshape((-1,) + piece.shape[1:])


def swap(value, axis, bit):
    return lax.ppermute(value, axis, [(i, i ^ bit) for i in range(lax.axis_size(axis))])


def from_owner(value, owner_id):
    across, along = lax.axis_size("x"), lax.axis_size("z")
    piece = split(value, "x", owner_id // along % across)
    piece = split(piece, "z", owner_id % along)
    if lax.axis_size("yh") > 1:
        other = swap(piece, "yh", 1)
        same = lax.axis_index("yh") == owner_id // (across * along)
        piece = jnp.where(same, piece, other)
    return piece


def sum_over(part, axis, kind):
    terms = lax.all_to_all(part, axis, 0, 0, tiled=True)
    return jnp.sum(terms.astype(f32), axis=0).astype(kind)


def step(wavefield, slowness, block_inverse, block_lengths, slab_owner, shot_position):
    counts = tuple(lax.axis_size(name) for name in FREQ_AXES)
    freq_total = math.prod(counts)
    cut_count = lax.axis_size("yl") * lax.axis_size("core")
    row_count, extent_y = wavefield.shape[2], wavefield.shape[3]
    extent_x = row_count * cut_count
    base = extent_y // RADIX
    freq_index = lax.axis_index(FREQ_AXES)
    cut_index = lax.axis_index(CUT_AXES)
    device = cut_index.reshape(1).astype(jnp.int32)
    angular = (
        2.0 * math.pi * (band_low + band_width * (freq_index.astype(f32) + 0.5) / freq_total)
    )
    inverse, turn = dft_tables(extent_y)
    turn_rows = turn[:, :base]
    turn_here = lax.dynamic_slice_in_dim(turn, cut_index * base, base, 1).T
    turn_cols = turn_rows.T
    chunk = jax.ShapeDtypeStruct((2 * row_count, base), bf16)

    spectrum = call(
        lines_forward_kernel,
        [chunk] * RADIX,
        [pltpu.VMEM((RADIX, row_count, 2 * base), bf16)],
        device, wavefield[0], inverse, turn_rows,
        scalars=1,
    )
    columns = rotate(spectrum, CUT_AXES)

    prop_re, prop_im = propagator(angular, cut_index, extent_x, extent_y)
    rows_x = cut_index * row_count + jnp.arange(row_count, dtype=jnp.int32)
    offset_x = (rows_x - shot_position[0]).astype(f32) * grid_step
    offset_y = (jnp.arange(extent_y, dtype=jnp.int32) - shot_position[1]).astype(f32) * grid_step
    distance = jnp.sqrt(
        offset_x[None, :] ** 2 + offset_y[:, None] ** 2 + depth_step * depth_step
    )
    ray = angular * slow_ref * distance
    level = 1.0 / math.sqrt(freq_total)
    cos_r, sin_r = cos_sin(ray)
    cos_r, sin_r = cos_r * level, sin_r * level
    owner_id = slab_owner[0]
    pieces = counts[1] * counts[2] * 16
    joined = jnp.concatenate([slowness[0].T, block_inverse[0].reshape(-1, row_count)], axis=0)
    filled = joined.shape[0]
    joined = jnp.pad(joined, ((0, -filled % pieces), (0, 0)))
    share = join(from_owner(joined, owner_id), "z")
    restored = call(
        across_kernel,
        [chunk] * RADIX,
        [
            pltpu.VMEM((RADIX, 2 * row_count, base), bf16),
            pltpu.VMEM((RADIX, 2 * row_count, base), f32),
            pltpu.VMEM(prop_re.shape, f32),
            pltpu.VMEM(prop_im.shape, f32),
            pltpu.SemaphoreType.DMA((2,)),
        ],
        *columns, inverse, turn_here, prop_re, prop_im,
        later=2,
    )
    row_field = rotate(restored, CUT_AXES)

    share, _ = lax.optimization_barrier((share, restored[0]))
    joined = join(share, "x")
    mine = joined[extent_y:filled]
    other = swap(mine, "core", 1)
    first = lax.axis_index("core") == 0
    operators = jnp.concatenate(
        [jnp.where(first, mine, other), jnp.where(first, other, mine)], axis=0
    )
    operators = join(operators, "yl")
    shape = block_inverse.shape
    matrices = operators.reshape((cut_count,) + shape[1:])
    matrices = jnp.pad(matrices, ((0, 0),) * 4 + ((0, -shape[4] % 128),))
    lengths = lax.dynamic_index_in_dim(block_lengths, owner_id, 0, keepdims=False)
    starts = jnp.cumsum(lengths) - lengths
    phases = angular * depth_step * (joined[:extent_y].astype(f32) - slow_ref)
    cos_u, sin_u = cos_sin(phases)

    late = (cos_u, sin_u, matrices, cos_r, sin_r)
    part = call(
        lines_inverse_kernel,
        jax.ShapeDtypeStruct(
            (counts[1], counts[0], counts[2], extent_y // freq_total, row_count), bf16
        ),
        [
            pltpu.VMEM((RADIX, 2 * base, row_count), f32),
            pltpu.VMEM((2, extent_y + shape[3], row_count), bf16),
            pltpu.VMEM((2, extent_y + shape[3], row_count), f32),
            *[pltpu.VMEM(value.shape, value.dtype) for value in late],
            pltpu.SemaphoreType.DMA((len(late),)),
        ],
        device, starts, lengths, *row_field, inverse, turn_cols, *late,
        scalars=3,
        later=len(late),
    )
    part = sum_over(part, "x", bf16)
    part = part.reshape((counts[0] * counts[2],) + part.shape[2:])
    image = sum_over(part, ("yh", "z"), f32)
    return image.T[None]


def solution(mesh):
    sizes = {"yh": 2, "x": 4, "z": 8, "yl": 4, "core": 2}
    if mesh.devices.size != math.prod(sizes.values()):
        sizes = {"yh": 1, "x": 1, "z": 1, "yl": 4, "core": 2}
    fine = Mesh(mesh.devices.reshape(tuple(sizes.values())), tuple(sizes))
    placed = (
        P(FREQ_AXES, None, CUT_AXES, None),
        P(FREQ_AXES, CUT_AXES, None),
        P(FREQ_AXES, None, CUT_AXES, None, None),
        P(),
        P(),
        P(),
    )
    return jax.shard_map(
        step, mesh=fine, in_specs=placed, out_specs=P(None, CUT_AXES, FREQ_AXES), check_vma=False
    )
```

```python
import math

import jax
import jax.numpy as jnp
import numpy as np
from jax import lax
from jax.experimental import pallas as pl
from jax.experimental.pallas import tpu as pltpu
from jax.sharding import Mesh, PartitionSpec as P

grid_step = 0.0125
depth_step = 0.02
slow_ref = 0.4
band_low = 5.0
band_width = 55.0

INTERPRET = False
FREQ_AXES = ("yh", "x", "z")
CUT_AXES = ("yl", "core")
RADIX = 8
f32 = jnp.float32
bf16 = jnp.bfloat16


def dft_tables(extent):
    base = extent // RADIX
    ids = np.arange(base)
    angle = 2.0 * np.pi / base * ((ids[:, None] * ids[None, :]) % base)
    cosine = np.cos(angle) / math.sqrt(base)
    sine = np.sin(angle) / math.sqrt(base)
    inverse = np.block([[cosine, -sine], [sine, cosine]])
    twists = 2.0 * np.pi / extent * (np.arange(RADIX)[:, None] * np.arange(extent)[None, :])
    turn = np.stack([np.cos(twists), np.sin(twists)], axis=1) / math.sqrt(RADIX)
    turn = turn.reshape(2 * RADIX, extent).astype(np.float32)
    return jnp.asarray(inverse, bf16), jnp.asarray(turn)


def fft4(parts, s):
    (r0, i0), (r1, i1), (r2, i2), (r3, i3) = parts
    ar, ai, br, bi = r0 + r2, i0 + i2, r0 - r2, i0 - i2
    cr, ci, dr, di = r1 + r3, i1 + i3, r1 - r3, i1 - i3
    if s > 0:
        one, three = (br - di, bi + dr), (br + di, bi - dr)
    else:
        one, three = (br + di, bi - dr), (br - di, bi + dr)
    return [(ar + cr, ai + ci), one, (ar - cr, ai - ci), three]


def fft8(parts, s):
    even = fft4(parts[0::2], s)
    odd = fft4(parts[1::2], s)
    half = math.sqrt(0.5)
    (r0, i0), (r1, i1), (r2, i2), (r3, i3) = odd
    if s > 0:
        turned = [
            (r0, i0),
            ((r1 - i1) * half, (i1 + r1) * half),
            (-i2, r2),
            ((r3 + i3) * -half, (r3 - i3) * half),
        ]
    else:
        turned = [
            (r0, i0),
            ((r1 + i1) * half, (i1 - r1) * half),
            (i2, -r2),
            ((i3 - r3) * half, (r3 + i3) * -half),
        ]
    low = [(e[0] + t[0], e[1] + t[1]) for e, t in zip(even, turned)]
    high = [(e[0] - t[0], e[1] - t[1]) for e, t in zip(even, turned)]
    return low + high


def twist(value, cosine, sine, s):
    real, imag = value
    if sine is None:
        return (real * cosine, imag * cosine)
    if s > 0:
        return (real * cosine - imag * sine, imag * cosine + real * sine)
    return (real * cosine + imag * sine, imag * cosine - real * sine)


def fetch(sources, targets, done):
    copies = [
        pltpu.make_async_copy(source, target, done.at[i])
        for i, (source, target) in enumerate(zip(sources, targets))
    ]
    for copy in copies:
        copy.start()
    return copies


def lines_forward_kernel(me, field, table, turn, *outs_mid):
    outs, mid = outs_mid[:RADIX], outs_mid[RADIX]
    rows, base = mid.shape[1], mid.shape[2] // 2

    def step(tile, carry):
        at = pl.ds(pl.multiple_of(tile * 16, 16), 16)
        for lane in range(0, base, 128):
            parts = []
            for a in range(RADIX):
                here = pl.ds(a * base + lane, 128)
                parts.append((field[0, at, here].astype(f32), field[1, at, here].astype(f32)))
            for k, value in enumerate(fft8(parts, -1)):
                cosine = turn[2 * k : 2 * k + 1, lane : lane + 128] if k else RADIX**-0.5
                sine = turn[2 * k + 1 : 2 * k + 2, lane : lane + 128] if k else None
                real, imag = twist(value, cosine, sine, -1)
                mid[k, at, pl.ds(lane, 128)] = real.astype(bf16)
                mid[k, at, pl.ds(base + lane, 128)] = imag.astype(bf16)
        return carry

    lax.fori_loop(0, rows // 16, step, 0)
    for d, out in enumerate(outs):
        both = jnp.dot(mid[(me[0] + d) % RADIX], table[...], preferred_element_type=f32)
        out[:rows] = both[:, :base].astype(bf16)
        out[rows:] = both[:, base:].astype(bf16)


def across_kernel(*refs):
    fields, refs = refs[:RADIX], refs[RADIX:]
    table, turn = refs[:2]
    later, refs = refs[2:4], refs[4:]
    outs, (mid, back, prop_re, prop_im, done) = refs[:RADIX], refs[RADIX:]
    copies = fetch(later, (prop_re, prop_im), done)
    base, cols = prop_re.shape[1], prop_re.shape[2]

    def fore(tile, carry):
        at = pl.multiple_of(tile * 16, 16)
        for lane in range(0, cols, 128):
            here = pl.ds(lane, 128)
            parts = []
            for field in fields:
                parts.append(
                    (
                        field[pl.ds(at, 16), here].astype(f32),
                        field[pl.ds(base + at, 16), here].astype(f32),
                    )
                )
            for k, value in enumerate(fft8(parts, 1)):
                cosine = turn[pl.ds(at, 16), 2 * k : 2 * k + 1] if k else RADIX**-0.5
                sine = turn[pl.ds(at, 16), 2 * k + 1 : 2 * k + 2] if k else None
                real, imag = twist(value, cosine, sine, -1)
                mid[k, pl.ds(at, 16), here] = real.astype(bf16)
                mid[k, pl.ds(base + at, 16), here] = (-imag).astype(bf16)
        return carry

    lax.fori_loop(0, base // 16, fore, 0)
    for copy in copies:
        copy.wait()

    def waves(step, carry):
        for k in (2 * step, 2 * step + 1):
            both = jnp.dot(table[...], mid[k], preferred_element_type=f32)
            real, minus = both[:base], both[base:]
            p_re, p_im = prop_re[k], prop_im[k]
            mid[k, :base] = (real * p_re + minus * p_im).astype(bf16)
            mid[k, base:] = (real * p_im - minus * p_re).astype(bf16)
            back[k] = jnp.dot(table[...], mid[k], preferred_element_type=f32)
        return carry

    lax.fori_loop(0, RADIX // 2, waves, 0)

    def aft(tile, carry):
        at = pl.multiple_of(tile * 16, 16)
        for lane in range(0, cols, 128):
            here = pl.ds(lane, 128)
            parts = []
            for k in range(RADIX):
                cosine = turn[pl.ds(at, 16), 2 * k : 2 * k + 1] if k else RADIX**-0.5
                sine = turn[pl.ds(at, 16), 2 * k + 1 : 2 * k + 2] if k else None
                value = (back[k, pl.ds(at, 16), here], back[k, pl.ds(base + at, 16), here])
                parts.append(twist(value, cosine, sine, 1))
            for out, (real, imag) in zip(outs, fft8(parts, 1)):
                out[pl.ds(at, 16), here] = real.astype(bf16)
                out[pl.ds(base + at, 16), here] = imag.astype(bf16)
        return carry

    lax.fori_loop(0, base // 16, aft, 0)


def lines_inverse_kernel(me, starts, lengths, *refs):
    fields, refs = refs[:RADIX], refs[RADIX:]
    table, turn = refs[:2]
    later, (out, back, turned, final), held, done = refs[2:7], refs[7:11], refs[11:16], refs[16]
    cos_u, sin_u, matrices, cos_r, sin_r = held
    copies = fetch(later, held, done)
    rows, base = fields[0].shape[0] // 2, fields[0].shape[1]
    cuts, _, share, capacity = matrices.shape[:4]
    reach = capacity + 16
    tail = pl.ds(RADIX * base, turned.shape[1] - RADIX * base)
    turned[:, tail, :] = jnp.zeros((2, tail.size, rows), bf16)
    final[:, tail, :] = jnp.zeros((2, tail.size, rows), f32)
    for d, field in enumerate(fields):
        first = lax.dot_general(
            table[:, :base], field[:rows], (((1,), (1,)), ((), ())), preferred_element_type=f32
        )
        second = lax.dot_general(
            table[:, base:], field[rows:], (((1,), (1,)), ((), ())), preferred_element_type=f32
        )
        back[(me[0] + RADIX - d) % RADIX] = first + second
    for copy in copies:
        copy.wait()

    def aft(tile, carry):
        at = pl.multiple_of(tile * 16, 16)
        for lane in range(0, rows, 128):
            here = pl.ds(lane, 128)
            parts = []
            for k in range(RADIX):
                cosine = turn[pl.ds(at, 16), 2 * k : 2 * k + 1] if k else RADIX**-0.5
                sine = turn[pl.ds(at, 16), 2 * k + 1 : 2 * k + 2] if k else None
                value = (back[k, pl.ds(at, 16), here], back[k, pl.ds(base + at, 16), here])
                parts.append(twist(value, cosine, sine, 1))
            for a, (real, imag) in enumerate(fft8(parts, 1)):
                cell = pl.ds(a * base + at, 16)
                cosine, sine = cos_u[cell, here], sin_u[cell, here]
                u_re = (real * cosine - imag * sine).astype(bf16)
                u_im = (real * sine + imag * cosine).astype(bf16)
                turned[0, cell, here] = u_re
                turned[1, cell, here] = u_im
                final[0, cell, here] = u_re.astype(f32)
                final[1, cell, here] = u_im.astype(f32)
        return carry

    lax.fori_loop(0, base // 16, aft, 0)

    lanes = matrices.shape[4]
    spot = lax.broadcasted_iota(jnp.int32, (capacity, lanes), 0)
    mate = lax.broadcasted_iota(jnp.int32, (capacity, lanes), 1)

    def some_blocks(cut, carry):
        cells, changes = [], []
        for one in range(share):
            c = cut * share + one
            start, length = starts[c], lengths[c]
            cell = pl.ds(pl.multiple_of(start // 16 * 16, 16), reach)
            inside = jnp.maximum(spot, mate) < length
            parts = []
            for part in range(2):
                value = jnp.where(inside, matrices[cut, part, one].astype(f32), 0.0)
                value = jnp.concatenate([value, jnp.zeros((reach - capacity, lanes), f32)], axis=0)
                value = pltpu.roll(pltpu.roll(value, start % 16, 0), start % 16, 1)
                parts.append(value[:, :reach].astype(bf16))
            both = jnp.concatenate(parts, axis=0)
            by_re = jnp.dot(both, turned[0, cell, :], preferred_element_type=f32)
            by_im = jnp.dot(both, turned[1, cell, :], preferred_element_type=f32)
            cells.append(cell)
            changes.append((by_re[:reach] - by_im[reach:], by_re[reach:] + by_im[:reach]))
        for cell, change in zip(cells, changes):
            final[0, cell, :] += change[0]
            final[1, cell, :] += change[1]
        return carry

    lax.fori_loop(0, cuts, some_blocks, 0)

    def image(tile, carry):
        cell = pl.ds(pl.multiple_of(tile * 16, 16), 16)
        across, _, along, piece = out.shape[:4]
        owner, place = tile * 16 // piece, tile * 16 % piece
        spot = pl.ds(pl.multiple_of(place, 16), 16)
        out[owner // along % across, owner // (along * across), owner % along, spot, :] = (
            final[0, cell, :] * cos_r[cell, :] - final[1, cell, :] * sin_r[cell, :]
        ).astype(bf16)
        return carry

    lax.fori_loop(0, RADIX * base // 16, image, 0, unroll=4)


def call(kernel, out_shape, scratch, *operands, scalars=0, later=0):
    anywhere = pl.BlockSpec(memory_space=pl.ANY)
    smem = pl.BlockSpec(memory_space=pltpu.SMEM)
    vmem = pl.BlockSpec(memory_space=pltpu.VMEM)
    return pl.pallas_call(
        kernel,
        out_shape=out_shape,
        in_specs=[smem] * scalars
        + [vmem] * (len(operands) - scalars - later)
        + [anywhere] * later,
        out_specs=jax.tree.map(lambda _: vmem, out_shape),
        scratch_shapes=scratch,
        interpret=INTERPRET,
    )(*operands)


def cos_sin(angle):
    quarters = jnp.round(angle * (2.0 / math.pi))
    rest = angle - quarters * 1.5703125
    rest = rest - quarters * 4.837512969970703125e-4
    rest = rest - quarters * 7.549789948768648e-8
    square = rest * rest
    sine = ((-1.9515295891e-4 * square + 8.3321608736e-3) * square - 1.6666654611e-1) * square
    sine = sine * rest + rest
    cosine = (2.443315711809948e-5 * square - 1.388731625493765e-3) * square
    cosine = (cosine + 4.166664568298827e-2) * (square * square) - 0.5 * square + 1.0
    count = quarters.astype(jnp.int32)
    odd = (count & 1) != 0
    first = jnp.where(odd, sine, cosine)
    second = jnp.where(odd, cosine, sine)
    return (
        jnp.where(((count + 1) & 2) != 0, -first, first),
        jnp.where((count & 2) != 0, -second, second),
    )


def wave_numbers(indices, extent):
    signed = jnp.where(indices < extent // 2, indices, indices - extent)
    return signed.astype(f32) * (2.0 * math.pi / (extent * grid_step))


def propagator(angular, cut_index, extent_x, extent_y):
    cross_ids = (
        jnp.arange(RADIX, dtype=jnp.int32)[:, None]
        + RADIX * jnp.arange(extent_x // RADIX, dtype=jnp.int32)[None, :]
    )
    line_ids = cut_index + RADIX * jnp.arange(extent_y // RADIX, dtype=jnp.int32)
    wave_x = wave_numbers(cross_ids, extent_x)
    wave_y = wave_numbers(line_ids, extent_y)
    vertical = (angular * slow_ref) ** 2 - wave_x[:, :, None] ** 2 - wave_y[None, None, :] ** 2
    root_abs = jnp.sqrt(jnp.abs(vertical))
    cosine, sine = cos_sin(root_abs * depth_step)
    real_part = jnp.where(vertical > 0, cosine, jnp.exp(-root_abs * depth_step))
    imag_part = jnp.where(vertical > 0, sine, jnp.zeros_like(root_abs))
    return (real_part, imag_part)


def rotate(values, axes):
    size = math.prod(lax.axis_size(axis) for axis in axes)
    got = [values[0]]
    for d in range(1, size):
        got.append(lax.ppermute(values[d], axes, [(i, (i + d) % size) for i in range(size)]))
    return got


def split(value, axis, owner):
    size = lax.axis_size(axis)
    shaped = value.reshape((size, value.shape[0] // size) + value.shape[1:])
    shaped = lax.all_to_all(shaped, axis, 0, 0)
    return lax.dynamic_index_in_dim(shaped, owner, 0, keepdims=False)


def join(piece, axis):
    copies = jnp.broadcast_to(piece[None], (lax.axis_size(axis),) + piece.shape)
    copies = lax.all_to_all(copies, axis, 0, 0)
    return copies.reshape((-1,) + piece.shape[1:])


def swap(value, axis, bit):
    return lax.ppermute(value, axis, [(i, i ^ bit) for i in range(lax.axis_size(axis))])


def from_owner(value, owner_id):
    across, along = lax.axis_size("x"), lax.axis_size("z")
    piece = split(value, "x", owner_id // along % across)
    piece = split(piece, "z", owner_id % along)
    if lax.axis_size("yh") > 1:
        other = swap(piece, "yh", 1)
        same = lax.axis_index("yh") == owner_id // (across * along)
        piece = jnp.where(same, piece, other)
    return piece


def sum_over(part, axis, kind):
    terms = lax.all_to_all(part, axis, 0, 0, tiled=True)
    return jnp.sum(terms.astype(f32), axis=0).astype(kind)


def step(wavefield, slowness, block_inverse, block_lengths, slab_owner, shot_position):
    counts = tuple(lax.axis_size(name) for name in FREQ_AXES)
    freq_total = math.prod(counts)
    cut_count = lax.axis_size("yl") * lax.axis_size("core")
    row_count, extent_y = wavefield.shape[2], wavefield.shape[3]
    extent_x = row_count * cut_count
    base = extent_y // RADIX
    freq_index = lax.axis_index(FREQ_AXES)
    cut_index = lax.axis_index(CUT_AXES)
    device = cut_index.reshape(1).astype(jnp.int32)
    angular = (
        2.0 * math.pi * (band_low + band_width * (freq_index.astype(f32) + 0.5) / freq_total)
    )
    inverse, turn = dft_tables(extent_y)
    turn_rows = turn[:, :base]
    turn_here = lax.dynamic_slice_in_dim(turn, cut_index * base, base, 1).T
    turn_cols = turn_rows.T
    chunk = jax.ShapeDtypeStruct((2 * row_count, base), bf16)

    spectrum = call(
        lines_forward_kernel,
        [chunk] * RADIX,
        [pltpu.VMEM((RADIX, row_count, 2 * base), bf16)],
        device, wavefield[0], inverse, turn_rows,
        scalars=1,
    )
    columns = rotate(spectrum, CUT_AXES)

    prop_re, prop_im = propagator(angular, cut_index, extent_x, extent_y)
    rows_x = cut_index * row_count + jnp.arange(row_count, dtype=jnp.int32)
    offset_x = (rows_x - shot_position[0]).astype(f32) * grid_step
    offset_y = (jnp.arange(extent_y, dtype=jnp.int32) - shot_position[1]).astype(f32) * grid_step
    distance = jnp.sqrt(
        offset_x[None, :] ** 2 + offset_y[:, None] ** 2 + depth_step * depth_step
    )
    ray = angular * slow_ref * distance
    level = 1.0 / math.sqrt(freq_total)
    cos_r, sin_r = cos_sin(ray)
    cos_r, sin_r = cos_r * level, sin_r * level
    owner_id = slab_owner[0]
    pieces = counts[1] * counts[2] * 16
    joined = jnp.concatenate([slowness[0].T, block_inverse[0].reshape(-1, row_count)], axis=0)
    filled = joined.shape[0]
    joined = jnp.pad(joined, ((0, -filled % pieces), (0, 0)))
    share = join(from_owner(joined, owner_id), "z")
    restored = call(
        across_kernel,
        [chunk] * RADIX,
        [
            pltpu.VMEM((RADIX, 2 * row_count, base), bf16),
            pltpu.VMEM((RADIX, 2 * row_count, base), f32),
            pltpu.VMEM(prop_re.shape, f32),
            pltpu.VMEM(prop_im.shape, f32),
            pltpu.SemaphoreType.DMA((2,)),
        ],
        *columns, inverse, turn_here, prop_re, prop_im,
        later=2,
    )
    row_field = rotate(restored, CUT_AXES)

    share, _ = lax.optimization_barrier((share, restored[0]))
    joined = join(share, "x")
    operators = join(joined[extent_y:filled], "yl")
    other = swap(operators, "core", 1)
    first = lax.axis_index("core") == 0
    operators = jnp.stack(
        [
            value.reshape(lax.axis_size("yl"), -1, row_count)
            for value in (jnp.where(first, operators, other), jnp.where(first, other, operators))
        ],
        axis=1,
    )
    shape = block_inverse.shape
    matrices = operators.reshape((cut_count,) + shape[1:])
    matrices = jnp.pad(matrices, ((0, 0),) * 4 + ((0, -shape[4] % 128),))
    lengths = lax.dynamic_index_in_dim(block_lengths, owner_id, 0, keepdims=False)
    starts = jnp.cumsum(lengths) - lengths
    phases = angular * depth_step * (joined[:extent_y].astype(f32) - slow_ref)
    cos_u, sin_u = cos_sin(phases)

    late = (cos_u, sin_u, matrices, cos_r, sin_r)
    part = call(
        lines_inverse_kernel,
        jax.ShapeDtypeStruct(
            (counts[1], counts[0], counts[2], extent_y // freq_total, row_count), bf16
        ),
        [
            pltpu.VMEM((RADIX, 2 * base, row_count), f32),
            pltpu.VMEM((2, extent_y + shape[3], row_count), bf16),
            pltpu.VMEM((2, extent_y + shape[3], row_count), f32),
            *[pltpu.VMEM(value.shape, value.dtype) for value in late],
            pltpu.SemaphoreType.DMA((len(late),)),
        ],
        device, starts, lengths, *row_field, inverse, turn_cols, *late,
        scalars=3,
        later=len(late),
    )
    part = sum_over(part, "x", bf16)
    part = part.reshape((counts[0] * counts[2],) + part.shape[2:])
    image = sum_over(part, ("yh", "z"), f32)
    return image.T[None]


def solution(mesh):
    sizes = {"yh": 2, "x": 4, "z": 8, "yl": 4, "core": 2}
    if mesh.devices.size != math.prod(sizes.values()):
        sizes = {"yh": 1, "x": 1, "z": 1, "yl": 4, "core": 2}
    fine = Mesh(mesh.devices.reshape(tuple(sizes.values())), tuple(sizes))
    placed = (
        P(FREQ_AXES, None, CUT_AXES, None),
        P(FREQ_AXES, CUT_AXES, None),
        P(FREQ_AXES, None, CUT_AXES, None, None),
        P(),
        P(),
        P(),
    )
    return jax.shard_map(
        step, mesh=fine, in_specs=placed, out_specs=P(None, CUT_AXES, FREQ_AXES), check_vma=False
    )
```

```python
import math

import jax
import jax.numpy as jnp
import numpy as np
from jax import lax
from jax.experimental import pallas as pl
from jax.experimental.pallas import tpu as pltpu
from jax.sharding import Mesh, PartitionSpec as P

grid_step = 0.0125
depth_step = 0.02
slow_ref = 0.4
band_low = 5.0
band_width = 55.0

INTERPRET = False
FREQ_AXES = ("yh", "x", "z")
CUT_AXES = ("yl", "core")
RADIX = 8
f32 = jnp.float32
bf16 = jnp.bfloat16


def dft_tables(extent):
    base = extent // RADIX
    ids = np.arange(base)
    angle = 2.0 * np.pi / base * ((ids[:, None] * ids[None, :]) % base)
    cosine = np.cos(angle) / math.sqrt(base)
    sine = np.sin(angle) / math.sqrt(base)
    inverse = np.block([[cosine, -sine], [sine, cosine]])
    twists = 2.0 * np.pi / extent * (np.arange(RADIX)[:, None] * np.arange(extent)[None, :])
    turn = np.stack([np.cos(twists), np.sin(twists)], axis=1) / math.sqrt(RADIX)
    turn = turn.reshape(2 * RADIX, extent).astype(np.float32)
    return jnp.asarray(inverse, bf16), jnp.asarray(turn)


def fft4(parts, s):
    (r0, i0), (r1, i1), (r2, i2), (r3, i3) = parts
    ar, ai, br, bi = r0 + r2, i0 + i2, r0 - r2, i0 - i2
    cr, ci, dr, di = r1 + r3, i1 + i3, r1 - r3, i1 - i3
    if s > 0:
        one, three = (br - di, bi + dr), (br + di, bi - dr)
    else:
        one, three = (br + di, bi - dr), (br - di, bi + dr)
    return [(ar + cr, ai + ci), one, (ar - cr, ai - ci), three]


def fft8(parts, s):
    even = fft4(parts[0::2], s)
    odd = fft4(parts[1::2], s)
    half = math.sqrt(0.5)
    (r0, i0), (r1, i1), (r2, i2), (r3, i3) = odd
    if s > 0:
        turned = [
            (r0, i0),
            ((r1 - i1) * half, (i1 + r1) * half),
            (-i2, r2),
            ((r3 + i3) * -half, (r3 - i3) * half),
        ]
    else:
        turned = [
            (r0, i0),
            ((r1 + i1) * half, (i1 - r1) * half),
            (i2, -r2),
            ((i3 - r3) * half, (r3 + i3) * -half),
        ]
    low = [(e[0] + t[0], e[1] + t[1]) for e, t in zip(even, turned)]
    high = [(e[0] - t[0], e[1] - t[1]) for e, t in zip(even, turned)]
    return low + high


def twist(value, cosine, sine, s):
    real, imag = value
    if sine is None:
        return (real * cosine, imag * cosine)
    if s > 0:
        return (real * cosine - imag * sine, imag * cosine + real * sine)
    return (real * cosine + imag * sine, imag * cosine - real * sine)


def fetch(sources, targets, done):
    copies = [
        pltpu.make_async_copy(source, target, done.at[i])
        for i, (source, target) in enumerate(zip(sources, targets))
    ]
    for copy in copies:
        copy.start()
    return copies


def lines_forward_kernel(me, field, table, turn, *outs_mid):
    outs, mid = outs_mid[:RADIX], outs_mid[RADIX]
    rows, base = mid.shape[1], mid.shape[2] // 2

    def step(tile, carry):
        at = pl.ds(pl.multiple_of(tile * 16, 16), 16)
        for lane in range(0, base, 128):
            parts = []
            for a in range(RADIX):
                here = pl.ds(a * base + lane, 128)
                parts.append((field[0, at, here].astype(f32), field[1, at, here].astype(f32)))
            for k, value in enumerate(fft8(parts, -1)):
                cosine = turn[2 * k : 2 * k + 1, lane : lane + 128] if k else RADIX**-0.5
                sine = turn[2 * k + 1 : 2 * k + 2, lane : lane + 128] if k else None
                real, imag = twist(value, cosine, sine, -1)
                mid[k, at, pl.ds(lane, 128)] = real.astype(bf16)
                mid[k, at, pl.ds(base + lane, 128)] = imag.astype(bf16)
        return carry

    lax.fori_loop(0, rows // 16, step, 0)
    for d, out in enumerate(outs):
        both = jnp.dot(mid[(me[0] + d) % RADIX], table[...], preferred_element_type=f32)
        out[:rows] = both[:, :base].astype(bf16)
        out[rows:] = both[:, base:].astype(bf16)


def across_kernel(*refs):
    fields, refs = refs[:RADIX], refs[RADIX:]
    table, turn = refs[:2]
    later, refs = refs[2:4], refs[4:]
    outs, (mid, back, prop_re, prop_im, done) = refs[:RADIX], refs[RADIX:]
    copies = fetch(later, (prop_re, prop_im), done)
    base, cols = prop_re.shape[1], prop_re.shape[2]

    def fore(tile, carry):
        at = pl.multiple_of(tile * 16, 16)
        for lane in range(0, cols, 128):
            here = pl.ds(lane, 128)
            parts = []
            for field in fields:
                parts.append(
                    (
                        field[pl.ds(at, 16), here].astype(f32),
                        field[pl.ds(base + at, 16), here].astype(f32),
                    )
                )
            for k, value in enumerate(fft8(parts, 1)):
                cosine = turn[pl.ds(at, 16), 2 * k : 2 * k + 1] if k else RADIX**-0.5
                sine = turn[pl.ds(at, 16), 2 * k + 1 : 2 * k + 2] if k else None
                real, imag = twist(value, cosine, sine, -1)
                mid[k, pl.ds(at, 16), here] = real.astype(bf16)
                mid[k, pl.ds(base + at, 16), here] = (-imag).astype(bf16)
        return carry

    lax.fori_loop(0, base // 16, fore, 0)
    for copy in copies:
        copy.wait()

    def waves(step, carry):
        for k in (2 * step, 2 * step + 1):
            both = jnp.dot(table[...], mid[k], preferred_element_type=f32)
            real, minus = both[:base], both[base:]
            p_re, p_im = prop_re[k], prop_im[k]
            mid[k, :base] = (real * p_re + minus * p_im).astype(bf16)
            mid[k, base:] = (real * p_im - minus * p_re).astype(bf16)
            back[k] = jnp.dot(table[...], mid[k], preferred_element_type=f32)
        return carry

    lax.fori_loop(0, RADIX // 2, waves, 0)

    def aft(tile, carry):
        at = pl.multiple_of(tile * 16, 16)
        for lane in range(0, cols, 128):
            here = pl.ds(lane, 128)
            parts = []
            for k in range(RADIX):
                cosine = turn[pl.ds(at, 16), 2 * k : 2 * k + 1] if k else RADIX**-0.5
                sine = turn[pl.ds(at, 16), 2 * k + 1 : 2 * k + 2] if k else None
                value = (back[k, pl.ds(at, 16), here], back[k, pl.ds(base + at, 16), here])
                parts.append(twist(value, cosine, sine, 1))
            for out, (real, imag) in zip(outs, fft8(parts, 1)):
                out[pl.ds(at, 16), here] = real.astype(bf16)
                out[pl.ds(base + at, 16), here] = imag.astype(bf16)
        return carry

    lax.fori_loop(0, base // 16, aft, 0)


def lines_inverse_kernel(me, starts, lengths, *refs):
    fields, refs = refs[:RADIX], refs[RADIX:]
    table, turn = refs[:2]
    later, (out, back, turned, final), held, done = refs[2:7], refs[7:11], refs[11:16], refs[16]
    cos_u, sin_u, matrices, cos_r, sin_r = held
    copies = fetch(later, held, done)
    rows, base = fields[0].shape[0] // 2, fields[0].shape[1]
    cuts, _, share, capacity = matrices.shape[:4]
    reach = capacity + 16
    tail = pl.ds(RADIX * base, turned.shape[1] - RADIX * base)
    turned[:, tail, :] = jnp.zeros((2, tail.size, rows), bf16)
    final[:, tail, :] = jnp.zeros((2, tail.size, rows), f32)
    for d, field in enumerate(fields):
        first = lax.dot_general(
            table[:, :base], field[:rows], (((1,), (1,)), ((), ())), preferred_element_type=f32
        )
        second = lax.dot_general(
            table[:, base:], field[rows:], (((1,), (1,)), ((), ())), preferred_element_type=f32
        )
        back[(me[0] + RADIX - d) % RADIX] = first + second
    for copy in copies:
        copy.wait()

    def aft(tile, carry):
        at = pl.multiple_of(tile * 16, 16)
        for lane in range(0, rows, 128):
            here = pl.ds(lane, 128)
            parts = []
            for k in range(RADIX):
                cosine = turn[pl.ds(at, 16), 2 * k : 2 * k + 1] if k else RADIX**-0.5
                sine = turn[pl.ds(at, 16), 2 * k + 1 : 2 * k + 2] if k else None
                value = (back[k, pl.ds(at, 16), here], back[k, pl.ds(base + at, 16), here])
                parts.append(twist(value, cosine, sine, 1))
            for a, (real, imag) in enumerate(fft8(parts, 1)):
                cell = pl.ds(a * base + at, 16)
                cosine, sine = cos_u[cell, here], sin_u[cell, here]
                u_re = (real * cosine - imag * sine).astype(bf16)
                u_im = (real * sine + imag * cosine).astype(bf16)
                turned[0, cell, here] = u_re
                turned[1, cell, here] = u_im
                final[0, cell, here] = u_re.astype(f32)
                final[1, cell, here] = u_im.astype(f32)
        return carry

    lax.fori_loop(0, base // 16, aft, 0)

    lanes = matrices.shape[4]
    spot = lax.broadcasted_iota(jnp.int32, (capacity, lanes), 0)
    mate = lax.broadcasted_iota(jnp.int32, (capacity, lanes), 1)

    def some_blocks(cut, carry):
        cells, changes = [], []
        for one in range(share):
            c = cut * share + one
            start, length = starts[c], lengths[c]
            cell = pl.ds(pl.multiple_of(start // 16 * 16, 16), reach)
            inside = jnp.maximum(spot, mate) < length
            parts = []
            for part in range(2):
                value = jnp.where(inside, matrices[cut, part, one].astype(f32), 0.0)
                value = jnp.concatenate([value, jnp.zeros((reach - capacity, lanes), f32)], axis=0)
                value = pltpu.roll(pltpu.roll(value, start % 16, 0), start % 16, 1)
                parts.append(value[:, :reach].astype(bf16))
            both = jnp.concatenate(parts, axis=0)
            by_re = jnp.dot(both, turned[0, cell, :], preferred_element_type=f32)
            by_im = jnp.dot(both, turned[1, cell, :], preferred_element_type=f32)
            cells.append(cell)
            changes.append((by_re[:reach] - by_im[reach:], by_re[reach:] + by_im[:reach]))
        for cell, change in zip(cells, changes):
            final[0, cell, :] += change[0]
            final[1, cell, :] += change[1]
        return carry

    lax.fori_loop(0, cuts, some_blocks, 0, unroll=2)

    def image(tile, carry):
        cell = pl.ds(pl.multiple_of(tile * 16, 16), 16)
        across, _, along, piece = out.shape[:4]
        owner, place = tile * 16 // piece, tile * 16 % piece
        spot = pl.ds(pl.multiple_of(place, 16), 16)
        out[owner // along % across, owner // (along * across), owner % along, spot, :] = (
            final[0, cell, :] * cos_r[cell, :] - final[1, cell, :] * sin_r[cell, :]
        ).astype(bf16)
        return carry

    lax.fori_loop(0, RADIX * base // 16, image, 0, unroll=8)


def call(kernel, out_shape, scratch, *operands, scalars=0, later=0):
    anywhere = pl.BlockSpec(memory_space=pl.ANY)
    smem = pl.BlockSpec(memory_space=pltpu.SMEM)
    vmem = pl.BlockSpec(memory_space=pltpu.VMEM)
    return pl.pallas_call(
        kernel,
        out_shape=out_shape,
        in_specs=[smem] * scalars
        + [vmem] * (len(operands) - scalars - later)
        + [anywhere] * later,
        out_specs=jax.tree.map(lambda _: vmem, out_shape),
        scratch_shapes=scratch,
        interpret=INTERPRET,
    )(*operands)


def cos_sin(angle):
    quarters = jnp.round(angle * (2.0 / math.pi))
    rest = angle - quarters * 1.5703125
    rest = rest - quarters * 4.837512969970703125e-4
    rest = rest - quarters * 7.549789948768648e-8
    square = rest * rest
    sine = ((-1.9515295891e-4 * square + 8.3321608736e-3) * square - 1.6666654611e-1) * square
    sine = sine * rest + rest
    cosine = (2.443315711809948e-5 * square - 1.388731625493765e-3) * square
    cosine = (cosine + 4.166664568298827e-2) * (square * square) - 0.5 * square + 1.0
    count = quarters.astype(jnp.int32)
    odd = (count & 1) != 0
    first = jnp.where(odd, sine, cosine)
    second = jnp.where(odd, cosine, sine)
    return (
        jnp.where(((count + 1) & 2) != 0, -first, first),
        jnp.where((count & 2) != 0, -second, second),
    )


def wave_numbers(indices, extent):
    signed = jnp.where(indices < extent // 2, indices, indices - extent)
    return signed.astype(f32) * (2.0 * math.pi / (extent * grid_step))


def propagator(angular, cut_index, extent_x, extent_y):
    cross_ids = (
        jnp.arange(RADIX, dtype=jnp.int32)[:, None]
        + RADIX * jnp.arange(extent_x // RADIX, dtype=jnp.int32)[None, :]
    )
    line_ids = cut_index + RADIX * jnp.arange(extent_y // RADIX, dtype=jnp.int32)
    wave_x = wave_numbers(cross_ids, extent_x)
    wave_y = wave_numbers(line_ids, extent_y)
    vertical = (angular * slow_ref) ** 2 - wave_x[:, :, None] ** 2 - wave_y[None, None, :] ** 2
    root_abs = jnp.sqrt(jnp.abs(vertical))
    cosine, sine = cos_sin(root_abs * depth_step)
    real_part = jnp.where(vertical > 0, cosine, jnp.exp(-root_abs * depth_step))
    imag_part = jnp.where(vertical > 0, sine, jnp.zeros_like(root_abs))
    return (real_part, imag_part)


def rotate(values, axes):
    size = math.prod(lax.axis_size(axis) for axis in axes)
    got = [values[0]]
    for d in range(1, size):
        got.append(lax.ppermute(values[d], axes, [(i, (i + d) % size) for i in range(size)]))
    return got


def split(value, axis, owner):
    size = lax.axis_size(axis)
    shaped = value.reshape((size, value.shape[0] // size) + value.shape[1:])
    shaped = lax.all_to_all(shaped, axis, 0, 0)
    return lax.dynamic_index_in_dim(shaped, owner, 0, keepdims=False)


def join(piece, axis):
    copies = jnp.broadcast_to(piece[None], (lax.axis_size(axis),) + piece.shape)
    copies = lax.all_to_all(copies, axis, 0, 0)
    return copies.reshape((-1,) + piece.shape[1:])


def swap(value, axis, bit):
    return lax.ppermute(value, axis, [(i, i ^ bit) for i in range(lax.axis_size(axis))])


def from_owner(value, owner_id):
    across, along = lax.axis_size("x"), lax.axis_size("z")
    piece = split(value, "x", owner_id // along % across)
    piece = split(piece, "z", owner_id % along)
    if lax.axis_size("yh") > 1:
        other = swap(piece, "yh", 1)
        same = lax.axis_index("yh") == owner_id // (across * along)
        piece = jnp.where(same, piece, other)
    return piece


def sum_over(part, axis, kind):
    terms = lax.all_to_all(part, axis, 0, 0, tiled=True)
    return jnp.sum(terms.astype(f32), axis=0).astype(kind)


def step(wavefield, slowness, block_inverse, block_lengths, slab_owner, shot_position):
    counts = tuple(lax.axis_size(name) for name in FREQ_AXES)
    freq_total = math.prod(counts)
    cut_count = lax.axis_size("yl") * lax.axis_size("core")
    row_count, extent_y = wavefield.shape[2], wavefield.shape[3]
    extent_x = row_count * cut_count
    base = extent_y // RADIX
    freq_index = lax.axis_index(FREQ_AXES)
    cut_index = lax.axis_index(CUT_AXES)
    device = cut_index.reshape(1).astype(jnp.int32)
    angular = (
        2.0 * math.pi * (band_low + band_width * (freq_index.astype(f32) + 0.5) / freq_total)
    )
    inverse, turn = dft_tables(extent_y)
    turn_rows = turn[:, :base]
    turn_here = lax.dynamic_slice_in_dim(turn, cut_index * base, base, 1).T
    turn_cols = turn_rows.T
    chunk = jax.ShapeDtypeStruct((2 * row_count, base), bf16)

    spectrum = call(
        lines_forward_kernel,
        [chunk] * RADIX,
        [pltpu.VMEM((RADIX, row_count, 2 * base), bf16)],
        device, wavefield[0], inverse, turn_rows,
        scalars=1,
    )
    columns = rotate(spectrum, CUT_AXES)

    prop_re, prop_im = propagator(angular, cut_index, extent_x, extent_y)
    rows_x = cut_index * row_count + jnp.arange(row_count, dtype=jnp.int32)
    cols_y = jnp.arange(extent_y, dtype=jnp.int32)
    offset_x = (rows_x - shot_position[0]).astype(f32) * grid_step
    offset_y = (cols_y - shot_position[1]).astype(f32) * grid_step
    distance = jnp.sqrt(offset_x[None, :] ** 2 + offset_y[:, None] ** 2 + depth_step * depth_step)
    level = 1.0 / math.sqrt(freq_total)
    cos_r, sin_r = cos_sin(angular * slow_ref * distance)
    cos_r, sin_r = cos_r * level, sin_r * level
    owner_id = slab_owner[0]
    pieces = counts[1] * counts[2] * 16
    joined = jnp.concatenate([slowness[0].T, block_inverse[0].reshape(-1, row_count)], axis=0)
    filled = joined.shape[0]
    joined = jnp.pad(joined, ((0, -filled % pieces), (0, 0)))
    share = join(from_owner(joined, owner_id), "z")
    restored = call(
        across_kernel,
        [chunk] * RADIX,
        [
            pltpu.VMEM((RADIX, 2 * row_count, base), bf16),
            pltpu.VMEM((RADIX, 2 * row_count, base), f32),
            pltpu.VMEM(prop_re.shape, f32),
            pltpu.VMEM(prop_im.shape, f32),
            pltpu.SemaphoreType.DMA((2,)),
        ],
        *columns, inverse, turn_here, prop_re, prop_im,
        later=2,
    )
    row_field = rotate(restored, CUT_AXES)

    share, _ = lax.optimization_barrier((share, restored[0]))
    joined = join(share, "x")
    joined, block_lengths = lax.optimization_barrier((joined, block_lengths))
    operators = join(joined[extent_y:filled], "yl")
    other = swap(operators, "core", 1)
    first = lax.axis_index("core") == 0
    operators = jnp.stack(
        [
            value.reshape(lax.axis_size("yl"), -1, row_count)
            for value in (jnp.where(first, operators, other), jnp.where(first, other, operators))
        ],
        axis=1,
    )
    shape = block_inverse.shape
    matrices = operators.reshape((cut_count,) + shape[1:])
    matrices = jnp.pad(matrices, ((0, 0),) * 4 + ((0, -shape[4] % 128),))
    lengths = lax.dynamic_index_in_dim(block_lengths, owner_id, 0, keepdims=False)
    starts = jnp.cumsum(lengths) - lengths
    phases = angular * depth_step * (joined[:extent_y].astype(f32) - slow_ref)
    cos_u, sin_u = cos_sin(phases)

    late = (cos_u, sin_u, matrices, cos_r, sin_r)
    part = call(
        lines_inverse_kernel,
        jax.ShapeDtypeStruct(
            (counts[1], counts[0], counts[2], extent_y // freq_total, row_count), bf16
        ),
        [
            pltpu.VMEM((RADIX, 2 * base, row_count), f32),
            pltpu.VMEM((2, extent_y + shape[3], row_count), bf16),
            pltpu.VMEM((2, extent_y + shape[3], row_count), f32),
            *[pltpu.VMEM(value.shape, value.dtype) for value in late],
            pltpu.SemaphoreType.DMA((len(late),)),
        ],
        device, starts, lengths, *row_field, inverse, turn_cols, *late,
        scalars=3,
        later=len(late),
    )
    part = sum_over(part, "x", bf16)
    part = part.reshape((counts[0] * counts[2],) + part.shape[2:])
    image = sum_over(part, ("yh", "z"), f32)
    return image.T[None]


def solution(mesh):
    sizes = {"yh": 2, "x": 4, "z": 8, "yl": 4, "core": 2}
    if mesh.devices.size != math.prod(sizes.values()):
        sizes = {"yh": 1, "x": 1, "z": 1, "yl": 4, "core": 2}
    fine = Mesh(mesh.devices.reshape(tuple(sizes.values())), tuple(sizes))
    placed = (
        P(FREQ_AXES, None, CUT_AXES, None),
        P(FREQ_AXES, CUT_AXES, None),
        P(FREQ_AXES, None, CUT_AXES, None, None),
        P(),
        P(),
        P(),
    )
    return jax.shard_map(
        step, mesh=fine, in_specs=placed, out_specs=P(None, CUT_AXES, FREQ_AXES), check_vma=False
    )
```
